32 devices in a mesh: dp: 2 (over y), slab: 16 (over z, x, core).
Axes of the slice: x: 2, y: 2, z: 4, core: 2. Of those that a mesh axis runs over, the one named last changes fastest.
Arguments:
- profiles: float32 [2, 4, 128, 128, 128], P('dp', None, 'slab'), may hold values from -4.5 to 4.5, as said below
- target_fields: float32 [2, 2, 128, 128, 128], P('dp', None, 'slab'), may hold values from -6 to 6
- lift_weight: float32 [4, 32], replicated, may hold values from -3 to 3
- local_weight: bfloat16 [32, 32], replicated, may hold values from -1 to 1
- local_bias: float32 [32], replicated, may hold values from -4 to 4
- output_weight: bfloat16 [32, 2], replicated, may hold values from -1 to 1
- output_bias: float32 [2], replicated, may hold values from -4 to 4
- mode_weight: float32 [2, 16, 16, 16, 1024], P(None, 'slab'), may hold values from -6 to 6
Outputs:
- predicted: float32 [2, 2, 128, 128, 128], P('dp', None, 'slab')
- mode_gradient: float32 [2, 16, 16, 16, 1024], P(None, 'slab', 'dp')
The draws below stay inside these ranges and needn't reach their ends.
Inputs may be any that keep to these rules, and one draw needn't show every extreme that they name: `profiles`: each input channel of each sample has zero mean over the grid, up to float32 rounding.
All inputs are finite; a program needn't handle non-finite values.
Results may differ from the reference program's by a relative error of at most 0.0061.
Values sent between devices are 32-bit elements; how exact they have to be, the bound alone decides.
A program may use at most 128 MiB of HBM per device.

```python
import jax
import jax.numpy as jnp
from jax import lax

C = 32
NIN = 4
NX = 128
NY = 128
NZ = 128
KX = 16
KY = 16
KZ = 16
SAMPLES = 2


def draw_profiles(key, part):
    shape = (SAMPLES, NIN, NX, NY, NZ)
    values = jnp.clip(jax.random.normal(key, shape, jnp.float32), -4.0, 4.0)
    return values - jnp.mean(values, axis=(2, 3, 4), keepdims=True)


def block_levels(rng, dims, cuts, smallest, largest):
    def one(position, blocks):
        draws = jax.random.uniform(jax.random.fold_in(jax.random.fold_in(rng, 6), position), (blocks,), jnp.float32, smallest / len(cuts), largest / len(cuts))
        return jnp.repeat(jnp.exp(draws), dims[position] // blocks).reshape((-1,) + (1,) * (len(dims) - position - 1))

    loudness = one(*cuts[0])
    for cut in cuts[1:]:
        loudness = loudness * one(*cut)
    return loudness


def centred(stream_key, shape, deviation, bound, pieces=(), kind=jnp.bfloat16):
    entries = jax.random.normal(stream_key, shape, jnp.float32) * deviation
    if len(pieces) > 0:
        entries = block_levels(stream_key, shape, pieces, -0.22, 0.18) * entries
    return jnp.clip(entries, min=-bound, max=bound).astype(kind)


def setup_inputs(seed: int = 0) -> dict:
    arg_keys = jax.random.split(jax.random.key(seed), 9)
    profiles = draw_profiles(jax.random.fold_in(arg_keys[8], 71), 0)
    target_fields = centred(arg_keys[1], (SAMPLES, 2, NX, NY, NZ), 1.0, 6.0, ((0, 2), (2, 16)), jnp.float32)
    lift_weight = centred(arg_keys[2], (NIN, C), NIN ** -0.5, 3.0, (), jnp.float32)
    local_weight = centred(arg_keys[3], (C, C), C ** -0.5, 1.0)
    local_bias = centred(arg_keys[4], (C,), 1.0, 4.0, (), jnp.float32)
    output_weight = centred(arg_keys[5], (C, 2), C ** -0.5, 1.0)
    output_bias = centred(arg_keys[6], (2,), 1.0, 4.0, (), jnp.float32)
    mode_weight = centred(arg_keys[7], (2, KY, KX, KZ, C * C), 1.0, 6.0, ((1, 16),), jnp.float32)
    return {"profiles": profiles, "target_fields": target_fields, "lift_weight": lift_weight, "local_weight": local_weight, "local_bias": local_bias, "output_weight": output_weight, "output_bias": output_bias, "mode_weight": mode_weight}


def mode_freqs(count):
    index_list = jnp.arange(count, dtype=jnp.int32)
    return jnp.where(index_list < count // 2, index_list, index_list - count).astype(jnp.int32)

def reference(profiles, target_fields, lift_weight, local_weight, local_bias, output_weight, output_bias, mode_weight):
    highest = lax.Precision.HIGHEST
    channels = lift_weight.shape[1]
    x_modes = jnp.mod(mode_freqs(KX), NX).astype(jnp.int32)
    y_modes = jnp.mod(mode_freqs(KY), NY).astype(jnp.int32)
    weights = mode_weight.reshape(2, KY, KX, KZ, channels, channels)
    w_complex = weights[0] + 1j * weights[1]
    doubling = jnp.where(jnp.arange(KZ) == 0, 1.0, 2.0).astype(jnp.float32)

    def retained(field):
        full_spectrum = jnp.fft.rfftn(field, axes=(1, 2, 3), norm='ortho')
        return (full_spectrum[:, x_modes][:, :, y_modes][:, :, :, :KZ], full_spectrum)

    def one_sample(running, inputs):
        sample, target = inputs
        lifted = jnp.einsum('ic,ixyz->cxyz', lift_weight, sample, precision=highest).astype(jnp.bfloat16)
        spectra, full_spectrum = retained(lifted.astype(jnp.float32))
        mixed = jnp.einsum('cpqk,qpkco->opqk', spectra, w_complex, precision=highest)
        placed = jnp.zeros(full_spectrum.shape, full_spectrum.dtype).at[:, x_modes[:, None], y_modes[None, :], :KZ].set(mixed)
        spectral = jnp.fft.irfftn(placed, s=(NX, NY, NZ), axes=(1, 2, 3), norm='ortho')
        columns = lifted.reshape(channels, -1)
        pre_act = spectral.reshape(channels, -1) + jnp.dot(local_weight.T, columns, preferred_element_type=jnp.float32) + local_bias[:, None]
        activated, slope_fn = jax.vjp(lambda value: jax.nn.gelu(value, approximate=True), pre_act)
        hidden = activated.astype(jnp.bfloat16)
        predicted = jnp.dot(output_weight.T, hidden, preferred_element_type=jnp.float32) + output_bias[:, None]
        misfit = predicted - target.reshape(2, -1)
        out_weights = output_weight.astype(jnp.float32)
        hidden_grad = out_weights[:, 0:1] * misfit[0:1] + out_weights[:, 1:2] * misfit[1:2]
        pre_grad, = slope_fn(hidden_grad)
        grad_spectra, unused_full = retained(pre_grad.reshape(channels, NX, NY, NZ))
        grad_spectra = grad_spectra * doubling[None, None, None, :]
        sample_grad = jnp.einsum('cpqk,opqk->qpkco', jnp.conj(spectra), grad_spectra)
        stacked = jnp.stack([jnp.real(sample_grad), jnp.imag(sample_grad)]).astype(jnp.float32)
        stacked = stacked.reshape(2, KY, KX, KZ, channels * channels)
        return (running + stacked, predicted.reshape(2, NX, NY, NZ))
    initial = jnp.zeros((2, KY, KX, KZ, channels * channels), jnp.float32)
    summed, predicted = lax.scan(one_sample, initial, (profiles, target_fields))
    return (predicted, summed)
```

```python
import functools
import math

import jax
import jax.numpy as jnp
import ml_dtypes
import numpy as np
from jax import lax
from jax.experimental import pallas as pl
from jax.experimental.pallas import tpu as pltpu
from jax.sharding import PartitionSpec as P

N = 128
K = 16
C = 32
NIN = 4
Q = 4
MESH = pl.DeviceIdType.MESH
BF = jnp.bfloat16
F32 = jnp.float32


def halves(table):
    table = np.asarray(table, np.float32)
    high = table.astype(ml_dtypes.bfloat16)
    low = (table - high.astype(np.float32)).astype(ml_dtypes.bfloat16)
    return high, low


def tables():
    freq = np.where(np.arange(K) < K // 2, np.arange(K), np.arange(K) - K)
    cell = np.arange(N)
    signed = 2.0 * np.pi * np.mod(freq[:, None] * cell[None, :], N) / N
    plain = 2.0 * np.pi * np.mod(np.arange(K)[:, None] * cell[None, :], N) / N
    norm = 1.0 / math.sqrt(N * N * N)
    doubling = np.where(np.arange(K) == 0, 1.0, 2.0)
    fy_h, fy_l = halves(np.concatenate([np.cos(signed), -np.sin(signed)], axis=0))
    fy_in = np.zeros((4 * K, 2 * N), ml_dtypes.bfloat16)
    fy_in[: 2 * K, :N], fy_in[: 2 * K, N:], fy_in[2 * K :, :N] = fy_h, fy_h, fy_l
    zc, zs = np.cos(plain).T, np.sin(plain).T

    def place(count):
        out = np.zeros((count, 2, N, 2, count, K))
        for c in range(count):
            out[c, 0, :, 0, c], out[c, 0, :, 1, c] = zc, -zs
            out[c, 1, :, 0, c], out[c, 1, :, 1, c] = zs, zc
        return out.reshape(count * 2 * N, 2 * count * K)

    back = np.zeros((2, 8, K, 8, 2, N))
    for c in range(8):
        wc, ws = doubling[:, None] * np.cos(plain), doubling[:, None] * np.sin(plain)
        back[0, c, :, c, 0], back[0, c, :, c, 1] = wc, ws
        back[1, c, :, c, 0], back[1, c, :, c, 1] = -ws, wc
    back = back.reshape(2 * 8 * K, 8 * 2 * N)
    iy = np.zeros((N, 3 * K), ml_dtypes.bfloat16)
    iy[:, : 2 * K] = halves(np.concatenate([np.cos(signed).T, -np.sin(signed).T], axis=1))[0]
    iy[:, 2 * K : 2 * K + 3] = 1.0
    fx = np.concatenate([np.cos(signed), -np.sin(signed)], axis=0) * norm
    ix = np.stack([np.repeat(np.cos(signed).T, K, axis=1), np.repeat(np.sin(signed).T, K, axis=1)]) * norm
    one = lambda value: np.asarray(value, np.float32).astype(ml_dtypes.bfloat16)
    pick = np.zeros((2, 2, NIN, K, 2, NIN, C))
    for part in range(2):
        for i in range(NIN):
            pick[:, part, i, :, part, i, :] = 1.0
    pick = one(pick.reshape(4 * NIN * K, 2 * NIN * C))
    rep = np.zeros((2, NIN, C, C, K))
    tile = np.zeros((C, K, 4, C))
    owner = np.zeros((N, C, C))
    for c in range(C):
        rep[:, :, c, c, :] = 1.0
        tile[c, :, :, c] = 1.0
        owner[c, c, :] = 1.0
    rep = one(rep.reshape(2 * NIN * C, C * K))
    tile = one(tile.reshape(C * K, 4 * C))
    owner = one(owner.reshape(N, C * C))
    hit = np.arange(N)[None, :] % K == np.arange(K)[:, None]
    first = np.arange(N) < N // 2
    masks = np.stack([hit, np.broadcast_to(np.tile(doubling, 8), (K, N)), np.broadcast_to(1.0 - 2.0 * first, (K, N))]).astype(np.float32)
    rows8 = one(np.repeat(np.eye(C), 8, axis=0))
    return {
        "fy_in": fy_in,
        "zp": np.concatenate(halves(place(NIN)), axis=1),
        "fx": np.concatenate(halves(fx), axis=0),
        "masks": masks,
        "pick": pick,
        "rows8": rows8,
        "cols8": np.ascontiguousarray(rows8.T),
        "rep": rep,
        "ix": np.stack(halves(ix)),
        "owner": owner,
        "iy": iy,
        "iz": halves(back)[0],
        "fy": fy_h,
        "zg": halves(place(8))[0],
        "tile": tile,
    }


FIRST = ("fy_in", "zp", "fx", "masks")


def split(value):
    high = value.astype(BF)
    return high, (value - high.astype(F32)).astype(BF)


def split3(value):
    high = value.astype(BF)
    rest = value - high.astype(F32)
    mid = rest.astype(BF)
    return high, mid, (rest - mid.astype(F32)).astype(BF)


def mm(left, right):
    return jnp.dot(left, right, preferred_element_type=F32)


def nt(left, right):
    return lax.dot_general(left, right, (((1,), (1,)), ((), ())), preferred_element_type=F32)


def right3(high, low, value):
    a, b = split(value)
    return mm(high, a) + mm(high, b) + mm(low, a)


def kernel(dp, slab, names, *refs):
    (prof_in, targ_in, modes_in, local, lift, outw_rows, bias, outb) = refs[:8]
    table_in = dict(zip(names, refs[8 : 8 + len(names)]))
    refs = refs[8 + len(names) :]
    pred_out, grad_out = refs[:2]
    refs = refs[2:]
    table = dict(zip(names, refs[: len(names)]))
    (prof, targ, modes, pred, grad,
     ubuf, sp, rp, sr, rr, wrow, lmat, lt_h, lt_l, kc, wl, pre, sums, spec, lost, bx, sm, rm, b_h,
     line_a, line_b, outw, acc, sg, rg, pm, xs, rx,
     in_sem, table_sem, pred_sem, grad_sem, p_send, p_recv, r_send, r_recv, w_send, w_recv, m_send, m_recv, g_send, g_recv, x_send, x_recv) = refs[len(names) :]
    me = lax.axis_index("slab")
    mine = lax.axis_index("dp")
    planes = prof.shape[1]
    share = K // dp
    some = planes // Q
    used = share * K

    barrier = pltpu.get_barrier_semaphore()
    for step in range(1, slab):
        pl.semaphore_signal(barrier, inc=1, device_id={"slab": lax.rem(me + step, slab)}, device_id_type=MESH)
    for step in range(1, dp):
        pl.semaphore_signal(barrier, inc=1, device_id={"dp": lax.rem(mine + step, dp)}, device_id_type=MESH)

    big = [pltpu.make_async_copy(prof_in, prof, in_sem.at[0]), pltpu.make_async_copy(modes_in, modes, in_sem.at[1]), pltpu.make_async_copy(targ_in, targ, in_sem.at[2])]
    small = {n: pltpu.make_async_copy(table_in[n], table[n], table_sem.at[i]) for i, n in enumerate(names)}
    big[0].start()
    for n in FIRST:
        small[n].start()
    big[1].start()
    for n in names:
        if n not in FIRST:
            small[n].start()
    big[2].start()

    def copies(source, target, send, recv, axis, here, count):
        out = []
        for step in range(1, count):
            peer = lax.rem(here + step, count)
            origin = lax.rem(here + count - step, count)
            going = pltpu.make_async_remote_copy(
                src_ref=source.at[peer], dst_ref=target.at[here], send_sem=send.at[peer], recv_sem=recv.at[here],
                device_id={axis: peer}, device_id_type=MESH)
            coming = pltpu.make_async_remote_copy(
                src_ref=source.at[peer], dst_ref=target.at[origin], send_sem=send.at[peer], recv_sem=recv.at[origin],
                device_id={axis: peer}, device_id_type=MESH)
            out.append((going, coming))
        return out

    def launch(pairs, source, target, here):
        for going, _ in pairs:
            going.start()
        target[pl.ds(here, 1)] = source[pl.ds(here, 1)]

    def finish(pairs):
        for going, coming in pairs:
            coming.wait_recv()
        for going, _ in pairs:
            going.wait_send()

    lane = lax.broadcasted_iota(jnp.int32, (C, N), 1)
    row = lax.broadcasted_iota(jnp.int32, (C, N), 0)

    big[0].wait()
    for n in FIRST:
        small[n].wait()

    @pl.loop(0, planes // 4)
    def _(turn):
        for sub in range(4):
            x = turn * 4 + sub
            rows = pl.ds(pl.multiple_of(x * K, K), K)
            for pair in range(NIN // 2):
                high, low = split(jnp.concatenate([prof[2 * pair, x], prof[2 * pair + 1, x]], axis=1))
                both = mm(table["fy_in"][...], jnp.concatenate([high, low], axis=0))
                u = both[: 2 * K] + both[2 * K :]
                for half in range(2):
                    i = 2 * pair + half
                    lanes = slice(half * N, (half + 1) * N)
                    ubuf[rows, 2 * i * N : (2 * i + 1) * N] = u[:K, lanes]
                    ubuf[rows, (2 * i + 1) * N : (2 * i + 2) * N] = u[K:, lanes]

    high, low = split(ubuf[:, : 2 * NIN * N])
    both = mm(high, table["zp"][...])
    v = both[:, :N] + both[:, N:] + mm(low, table["zp"][:, :N])
    for x in range(planes):
        sp[:, x, :] = v[x * K : (x + 1) * K, :]

    pl.semaphore_wait(barrier, slab + dp - 2)
    pairs = copies(sp, rp, p_send, p_recv, "slab", me, slab)
    launch(pairs, sp, rp, me)

    def groups(scalars):
        out = jnp.where(lane < 3 * C, scalars[2], scalars[3])
        out = jnp.where(lane < 2 * C, scalars[1], out)
        return jnp.where(lane < C, scalars[0], out)

    same = row == lax.rem(lane, C)
    for c in range(C):
        high, low = split(jnp.where(same, groups([lift[i, c] for i in range(NIN)]), 0.0))
        lmat[c * C : (c + 1) * C, :N] = high
        lmat[c * C : (c + 1) * C, N:] = low
    for t in range(C // 4):
        for i in range(NIN):
            high, low = split(jnp.where(same, groups([lift[i, 4 * t + j] for j in range(4)]), 0.0))
            lt_h[i * C : (i + 1) * C, t * N : (t + 1) * N] = high
            lt_l[i * C : (i + 1) * C, t * N : (t + 1) * N] = low
    for n in names:
        if n not in FIRST:
            small[n].wait()
    spread = mm(nt(table["rows8"][...], local[...]).astype(BF), table["cols8"][...])
    wide_lane = lax.broadcasted_iota(jnp.int32, (C * 8, 2 * N), 1)
    wide_row = lax.broadcasted_iota(jnp.int32, (C * 8, 2 * N), 0)
    kc[: C * 8, :] = jnp.where(lax.rem(wide_lane, 8) == lax.rem(wide_row, 8), spread, 0.0).astype(BF)
    kc[C * 8 :, :] = jnp.where(wide_lane[:C] // 8 == wide_row[:C], 1.0, 0.0).astype(BF)
    ones = jnp.ones((N, N), BF)

    def down(value):
        pieces = split3(jnp.where(row == lane, jnp.broadcast_to(value, (C, N)), 0.0))
        return mm(pieces[0], ones) + mm(pieces[1], ones) + mm(pieces[2], ones)

    for j in range(2):
        padded = jnp.concatenate([outw_rows[j : j + 1, :].astype(F32)] * 4, axis=1)
        outw[j] = 0.5 * down(padded)
    sums[...] = jnp.zeros_like(sums)

    def local_map(first, last):
        @pl.loop(first // 2, last // 2)
        def _(turn):
            for sub in range(2):
                step = turn * 2 + sub
                x, yb = step // 8, lax.rem(step, 8)
                sides = []
                for q in range(2):
                    rows = pl.ds(pl.multiple_of(yb * 16 + q * 8, 8), 8)
                    inputs = [prof[i, x, rows, :] for i in range(NIN)]
                    lifted = []
                    for c in range(C):
                        value = lift[0, c] * inputs[0]
                        for i in range(1, NIN):
                            value = value + lift[i, c] * inputs[i]
                        lifted.append(value)
                    sides.append(jnp.concatenate(lifted, axis=0).astype(BF))
                out = mm(kc[...], jnp.concatenate(sides, axis=1))
                pre[x, yb] = out[: C * 8]
                sums[sub] += out[C * 8 :]

    steps = planes * 8
    early = 24
    local_map(0, early)

    big[1].wait()
    for part in range(2):
        for block in range(2):
            rows = slice(block * N, (block + 1) * N)
            total = None
            for t in range(4):
                lanes = slice(t * 2 * N, (t + 1) * 2 * N)
                high, low = split(modes[part, rows, lanes])
                both = mm(high, lmat[lanes, :])
                both = both[:, :N] + both[:, N:] + mm(low, lmat[lanes, :N])
                total = both if total is None else total + both
            wl[part, rows, :] = total

    def weight_row(peer, send):
        return pltpu.make_async_remote_copy(
            src_ref=modes.at[0, pl.ds(0, 1), :], dst_ref=wrow, send_sem=send, recv_sem=w_recv,
            device_id={"slab": peer}, device_id_type=MESH)

    @pl.when(me == 0)
    def _():
        for step in range(1, slab):
            weight_row(step, w_send.at[step]).start()
        wrow[...] = modes[0, :1, :]

    finish(pairs)
    hit = table["masks"][0]
    y = table["fx"]
    y = right3(y[: 2 * K, :], y[2 * K :, :], rp[...].reshape(N, N))
    value = y[:K] + table["masks"][2] * pltpu.roll(y[K:], N // 2, 1)
    constant = (row[:K] == 0) & (lax.rem(lane[:K], K) == 0) & (me == 0)
    spec[...] = jnp.where(constant, 0.0, value)

    def expand(row_of, count):
        wide = jnp.concatenate([jnp.broadcast_to(row_of(p), (K, N)) * hit for p in range(count)], axis=0)
        both = mm(jnp.concatenate(split(wide), axis=1), table["pick"][...])
        return both[:, :N], both[:, N:]

    s_re, s_im = expand(lambda p: spec[p : p + 1, :], K)
    w_re, w_im = wl[0], wl[1]
    spread = []
    for value in (s_re * w_re - s_im * w_im, s_re * w_im + s_im * w_re):
        spread.append(mm(jnp.concatenate(split(value), axis=1), table["rep"][...]))
    keep = jnp.concatenate([hit] * K, axis=0)
    ix_h, ix_l = table["ix"][0], table["ix"][1]
    for og in range(4):
        lanes = slice(og * N, (og + 1) * N)
        re, im = split(spread[0][:, lanes] * keep), split(spread[1][:, lanes] * keep)

        def turned(a, value):
            return mm(ix_h[a], value[0]) + mm(ix_h[a], value[1]) + mm(ix_l[a], value[0])

        for part, out in enumerate((turned(0, re) - turned(1, im), turned(0, im) + turned(1, re))):
            for h in range(Q):
                for d in range(slab):
                    first = d * planes + h * some
                    sm[h, d, :, (2 * og + part) * N : (2 * og + part + 1) * N] = out[first : first + some]

    def moving(h):
        return copies(sm.at[h], rm.at[h], m_send.at[h], m_recv.at[h], "slab", me, slab)

    def leaving(h):
        return copies(sg.at[h], rg.at[h], g_send.at[h], g_recv.at[h], "slab", me, slab)

    launch(moving(0), sm.at[0], rm.at[0], me)
    local_map(early, steps)

    value = sums[0] + sums[1]
    pieces = split3(jnp.concatenate([value[:, :N] + value[:, N:], jnp.zeros((N - C, N), F32)], axis=0))
    flat = jnp.ones((8, N), BF)
    total = nt(flat, pieces[0]) + nt(flat, pieces[1]) + nt(flat, pieces[2])
    for q in range(slab):
        sr[q] = total[:1]
    more = copies(sr, rr, r_send, r_recv, "slab", me, slab)
    launch(more, sr, rr, me)
    for h in range(1, Q):
        launch(moving(h), sm.at[h], rm.at[h], me)

    @pl.when(me == 0)
    def _():
        for step in range(1, slab):
            weight_row(step, w_send.at[step]).wait_send()

    @pl.when(me != 0)
    def _():
        weight_row(0, w_send.at[0]).wait_recv()

    finish(more)
    total = rr[0]
    for q in range(1, slab):
        total = total + rr[q]
    lost[...] = total * jnp.where(me == 0, 1.0 / math.sqrt(N * N * N), 0.0).astype(F32)
    pieces = split3(jnp.broadcast_to(total * (1.0 / (N * N * N)), (8, N)))
    shift = mm(pieces[0], table["owner"][...]) + mm(pieces[1], table["owner"][...]) + mm(pieces[2], table["owner"][...])
    value = jnp.zeros((1, N), F32)
    for t in range(C * C // N):
        lanes = slice(t * N, (t + 1) * N)
        value = value + shift[:1, lanes] * wrow[:, lanes]
    value = value + pltpu.roll(value, 64, 1)
    moved = down(value + pltpu.roll(value, 32, 1))
    top = lax.broadcasted_iota(jnp.int32, (K, N), 0)
    for o in range(C):
        a, b, c = split3(jnp.broadcast_to(moved[o : o + 1, :] + bias[o], (K, N)))
        a, b, c = a.astype(F32), b.astype(F32), c.astype(F32)
        value = jnp.where(top == 0, a, jnp.where(top == 1, b, jnp.where(top == 2, c, 0.0)))
        bx[o // 2, :, (o % 2) * N : (o % 2 + 1) * N] = value.astype(BF)
    big[2].wait()

    c0 = math.sqrt(2.0 / math.pi)

    def lines(x, group, out):
        rows = pl.ds(pl.multiple_of(x * K, K), K)
        for sub in range(4):
            pair = group * 4 + sub
            blocks = []
            for half in range(2):
                b = b_h[pair * 2 + half, rows, :]
                blocks.append(jnp.concatenate([b[:, :N], b[:, N:]], axis=0))
            right = jnp.concatenate([jnp.concatenate(blocks, axis=1), bx[pair]], axis=0)
            out[sub] = mm(table["iy"][...], right)

    def activate(x, group, field):
        for yb in range(N // 16):
            ys = slice(yb * 16, (yb + 1) * 16)
            if group == 0:
                add = [jnp.zeros((16, N), F32)] * 2
            else:
                add = [acc[0, ys, :], acc[1, ys, :]]
            for sub in range(8):
                o = group * 8 + sub
                rows = slice(o * 8, (o + 1) * 8)
                base = jnp.concatenate([pre[x, yb, rows, :N], pre[x, yb, rows, N:]], axis=0)
                v = field[sub // 2, ys, (sub % 2) * N : (sub % 2 + 1) * N] + base
                a = c0 * v
                b = a * ((v * v) * 0.044715)
                t = jnp.tanh(a + b)
                p = 1.0 + t
                slope = p * (1.0 + (1.0 - t) * ((a + b) + (b + b)))
                pre[x, yb, rows, :N] = slope[:8]
                pre[x, yb, rows, N:] = slope[8:]
                hidden = (v * p).astype(BF).astype(F32)
                add = [add[j] + outw[j, o : o + 1, :] * hidden for j in range(2)]
            acc[0, ys, :] = add[0]
            acc[1, ys, :] = add[1]

    def pred_copy(x):
        return pltpu.make_async_copy(pred.at[:, x], pred_out.at[:, x], pred_sem.at[x])

    @pl.loop(0, Q)
    def _(h):
        finish(moving(h))
        block = pl.ds(pl.multiple_of(h * some * K, some * K), some * K)
        for og in range(4):
            high = jnp.concatenate([rm[h, :, x, og * 2 * N : (og + 1) * 2 * N] for x in range(some)], axis=0).astype(BF)
            value = mm(high, table["iz"][...]).astype(BF)
            for t in range(8):
                b_h[og * 8 + t, block, :] = value[:, t * 2 * N : (t + 1) * 2 * N]

        lines(h * some, 0, line_a)

        @pl.loop(h * some, (h + 1) * some)
        def _(x):
            for group in range(4):
                here, there = (line_a, line_b) if group % 2 == 0 else (line_b, line_a)
                if group < 3:
                    lines(x, group + 1, there)
                else:
                    lines(jnp.minimum(x + 1, (h + 1) * some - 1), 0, there)
                activate(x, group, here)
            for j in range(2):
                value = acc[j] + outb[j]
                pred[j, x] = value
                acc[j] = value - targ[j, x]
            pred_copy(x).start()
            rows = pl.ds(pl.multiple_of(x * K, K), K)
            for pair in range(C // 2):
                parts = []
                for half in range(2):
                    o = pair * 2 + half
                    w = [outw[j, o : o + 1, :] for j in range(2)]
                    pieces = []
                    for yb in range(N // 16):
                        ys = slice(yb * 16, (yb + 1) * 16)
                        slope = jnp.concatenate([pre[x, yb, o * 8 : (o + 1) * 8, :N], pre[x, yb, o * 8 : (o + 1) * 8, N:]], axis=0)
                        pieces.append(((w[0] * acc[0, ys, :] + w[1] * acc[1, ys, :]) * slope).astype(BF))
                    parts.append(jnp.concatenate(pieces, axis=0))
                u = mm(table["fy"][...], jnp.concatenate(parts, axis=1))
                for half in range(2):
                    at = (pair * 2 + half) * 2 * N
                    ubuf[rows, at : at + N] = u[:K, half * N : (half + 1) * N]
                    ubuf[rows, at + N : at + 2 * N] = u[K:, half * N : (half + 1) * N]

        for og in range(4):
            high, low = split(ubuf[block, og * 16 * N : (og + 1) * 16 * N])
            v = mm(high, table["zg"][...]) + mm(low, table["zg"][...])
            for x in range(some):
                sg[h, :, x, og * 2 * N : (og + 1) * 2 * N] = v[x * K : (x + 1) * K, :]
        launch(leaving(h), sg.at[h], rg.at[h], me)

    for h in range(Q):
        finish(leaving(h))
        for d in range(slab):
            first = d * planes + h * some
            pm[first : first + some, :] = rg[h, d]

    y = right3(table["fx"][: 2 * K, :], table["fx"][2 * K :, :], pm[...])
    twice = table["masks"][1]
    for og in range(4):
        re, im = slice(2 * og * N, (2 * og + 1) * N), slice((2 * og + 1) * N, (2 * og + 2) * N)
        out_re = (y[:K, re] - y[K:, im]) * twice
        out_im = (y[:K, im] + y[K:, re]) * twice
        for d in range(dp):
            ps = slice(d * share, (d + 1) * share)
            xs[d, :, re] = out_re[ps]
            xs[d, :, im] = out_im[ps]
    for d in range(dp):
        xs[d, :, 8 * N : 9 * N] = spec[d * share : (d + 1) * share, :]
        xs[d, :, 9 * N :] = jnp.broadcast_to(lost[...], (share, N)) if d == 0 else jnp.zeros((share, N), F32)

    pairs = copies(xs, rx, x_send, x_recv, "dp", mine, dp)
    for going, _ in pairs:
        going.start()

    def term(ref, d):
        s_re, s_im = expand(lambda p: ref[d, pl.ds(p, 1), 8 * N : 9 * N], share)
        g = []
        for part in range(2):
            total = None
            for og in range(4):
                at = (2 * og + part) * N
                wide = jnp.concatenate([jnp.broadcast_to(ref[d, pl.ds(p, 1), at : at + N], (K, N)) * hit for p in range(share)], axis=0)
                high, low = split(wide)
                weight = table["tile"][og * N : (og + 1) * N, :]
                value = mm(high, weight) + mm(low, weight)
                total = value if total is None else total + value
            g.append(total)
        pieces = split(jnp.broadcast_to(ref[d, pl.ds(0, 1), 9 * N :], (8, N)))
        gone = (mm(pieces[0], table["owner"][...]) + mm(pieces[1], table["owner"][...]))[:1, :]
        wide = [jnp.concatenate([g[part][:1, :]] * (C * C // N), axis=1) * gone for part in range(2)]
        return s_re * g[0] + s_im * g[1], s_re * g[1] - s_im * g[0], wide[0], wide[1]

    total = term(xs, mine)
    finish(pairs)
    for step in range(1, dp):
        total = [a + b for a, b in zip(total, term(rx, lax.rem(mine + step, dp)))]

    grads = [pltpu.make_async_copy(grad.at[part], grad_out.at[part], grad_sem.at[part]) for part in range(2)]
    for part in range(2):
        high, low = split(total[part])
        value = mm(jnp.concatenate([high, low], axis=1), jnp.concatenate([lt_h[...], lt_h[...]], axis=0)) + mm(high, lt_l[...])
        grad[part] = value
        grad[part, :1, :] = value[:1, :] + total[2 + part]
        grads[part].start()
    for part in range(2):
        grads[part].wait()
    for x in range(planes):
        pred_copy(x).wait()


def body(dp, slab, consts, profiles, target_fields, lift_weight, local_weight, local_bias, output_weight, output_bias, mode_weight):
    planes = profiles.shape[2]
    share = K // dp
    some = planes // Q
    vmem = pl.BlockSpec(memory_space=pltpu.VMEM)
    smem = pl.BlockSpec(memory_space=pltpu.SMEM)
    far = pl.BlockSpec(memory_space=pl.ANY)
    dma = pltpu.SemaphoreType.DMA
    buf = pltpu.VMEM
    names = tuple(consts)
    values = [jnp.asarray(consts[n]) for n in names]
    pred, grad = pl.pallas_call(
        functools.partial(kernel, dp, slab, names),
        out_shape=(jax.ShapeDtypeStruct((2, planes, N, N), F32), jax.ShapeDtypeStruct((2, share * K, C * C), F32)),
        in_specs=[far] * 3 + [vmem, smem, vmem, smem, smem] + [far] * len(names),
        out_specs=(far, far),
        scratch_shapes=[buf(v.shape, v.dtype) for v in values] + [
            buf((NIN, planes, N, N), F32),
            buf((2, planes, N, N), F32),
            buf((2, K * K, C * C), F32),
            buf((2, planes, N, N), F32),
            buf((2, share * K, C * C), F32),
            buf((planes * K, C * 2 * N), F32),
            buf((slab, planes, N), F32),
            buf((slab, planes, N), F32),
            buf((slab, 1, N), F32),
            buf((slab, 1, N), F32),
            buf((1, C * C), F32),
            buf((C * C, 2 * N), BF),
            buf((NIN * C, C * C), BF),
            buf((NIN * C, C * C), BF),
            buf((C * 8 + C, 2 * N), BF),
            buf((2, K * K, N), F32),
            buf((planes, N // 16, C * 8, 2 * N), F32),
            buf((2, C, 2 * N), F32),
            buf((K, N), F32),
            buf((1, N), F32),
            buf((C // 2, K, 2 * N), BF),
            buf((Q, slab, some, 8 * N), F32),
            buf((Q, slab, some, 8 * N), F32),
            buf((C, planes * K, 2 * N), BF),
            buf((4, N, 2 * N), F32),
            buf((4, N, 2 * N), F32),
            buf((2, C, N), F32),
            buf((2, N, N), F32),
            buf((Q, slab, some, 8 * N), F32),
            buf((Q, slab, some, 8 * N), F32),
            buf((N, 8 * N), F32),
            buf((dp, share, 10 * N), F32),
            buf((dp, share, 10 * N), F32),
            dma((3,)), dma((len(names),)), dma((planes,)), dma((2,)),
            dma((slab,)), dma((slab,)), dma((slab,)), dma((slab,)), dma((slab,)), dma(()),
            dma((Q, slab)), dma((Q, slab)), dma((Q, slab)), dma((Q, slab)), dma((dp,)), dma((dp,)),
        ],
        compiler_params=pltpu.CompilerParams(collective_id=0, has_side_effects=True, vmem_limit_bytes=56 << 20),
    )(profiles[0], target_fields[0], mode_weight.reshape(2, K * K, C * C), local_weight, lift_weight,
      output_weight.T, local_bias, output_bias, *values)
    return pred[None], grad.reshape(2, 1, share, K, C * C)


def solution(mesh):
    consts = tables()
    in_specs = (
        P("dp", None, "slab", None, None),
        P("dp", None, "slab", None, None),
        P(),
        P(),
        P(),
        P(),
        P(),
        P(None, "slab", None, None, None),
    )
    out_specs = (P("dp", None, "slab", None, None), P(None, "slab", "dp", None, None))

    def run(*args):
        return body(mesh.shape["dp"], mesh.shape["slab"], consts, *args)

    return jax.shard_map(run, mesh=mesh, in_specs=in_specs, out_specs=out_specs, check_vma=False)
```

```python
import functools
import math

import jax
import jax.numpy as jnp
import ml_dtypes
import numpy as np
from jax import lax
from jax.experimental import pallas as pl
from jax.experimental.pallas import tpu as pltpu
from jax.sharding import PartitionSpec as P

N = 128
K = 16
C = 32
NIN = 4
Q = 4
MESH = pl.DeviceIdType.MESH
BF = jnp.bfloat16
F32 = jnp.float32


def halves(table):
    table = np.asarray(table, np.float32)
    high = table.astype(ml_dtypes.bfloat16)
    low = (table - high.astype(np.float32)).astype(ml_dtypes.bfloat16)
    return high, low


def tables():
    freq = np.where(np.arange(K) < K // 2, np.arange(K), np.arange(K) - K)
    cell = np.arange(N)
    signed = 2.0 * np.pi * np.mod(freq[:, None] * cell[None, :], N) / N
    plain = 2.0 * np.pi * np.mod(np.arange(K)[:, None] * cell[None, :], N) / N
    norm = 1.0 / math.sqrt(N * N * N)
    doubling = np.where(np.arange(K) == 0, 1.0, 2.0)
    fy_h, fy_l = halves(np.concatenate([np.cos(signed), -np.sin(signed)], axis=0))
    fy_in = np.zeros((4 * K, 2 * N), ml_dtypes.bfloat16)
    fy_in[: 2 * K, :N], fy_in[: 2 * K, N:], fy_in[2 * K :, :N] = fy_h, fy_h, fy_l
    zc, zs = np.cos(plain).T, np.sin(plain).T

    def place(count):
        out = np.zeros((count, 2, N, 2, count, K))
        for c in range(count):
            out[c, 0, :, 0, c], out[c, 0, :, 1, c] = zc, -zs
            out[c, 1, :, 0, c], out[c, 1, :, 1, c] = zs, zc
        return out.reshape(count * 2 * N, 2 * count * K)

    back = np.zeros((2, 8, K, 8, 2, N))
    for c in range(8):
        wc, ws = doubling[:, None] * np.cos(plain), doubling[:, None] * np.sin(plain)
        back[0, c, :, c, 0], back[0, c, :, c, 1] = wc, ws
        back[1, c, :, c, 0], back[1, c, :, c, 1] = -ws, wc
    back = back.reshape(2 * 8 * K, 8 * 2 * N)
    iy = np.zeros((N, 3 * K), ml_dtypes.bfloat16)
    iy[:, : 2 * K] = halves(np.concatenate([np.cos(signed).T, -np.sin(signed).T], axis=1))[0]
    iy[:, 2 * K : 2 * K + 3] = 1.0
    fx = np.concatenate([np.cos(signed), -np.sin(signed)], axis=0) * norm
    ix = np.stack([np.repeat(np.cos(signed).T, K, axis=1), np.repeat(np.sin(signed).T, K, axis=1)]) * norm
    one = lambda value: np.asarray(value, np.float32).astype(ml_dtypes.bfloat16)
    pick = np.zeros((2, 2, NIN, K, 2, NIN, C))
    for part in range(2):
        for i in range(NIN):
            pick[:, part, i, :, part, i, :] = 1.0
    pick = one(pick.reshape(4 * NIN * K, 2 * NIN * C))
    rep = np.zeros((2, NIN, C, C, K))
    tile = np.zeros((C, K, 4, C))
    owner = np.zeros((N, C, C))
    for c in range(C):
        rep[:, :, c, c, :] = 1.0
        tile[c, :, :, c] = 1.0
        owner[c, c, :] = 1.0
    rep = one(rep.reshape(2 * NIN * C, C * K))
    tile = one(tile.reshape(C * K, 4 * C))
    owner = one(owner.reshape(N, C * C))
    hit = np.arange(N)[None, :] % K == np.arange(K)[:, None]
    first = np.arange(N) < N // 2
    masks = np.stack([hit, np.broadcast_to(np.tile(doubling, 8), (K, N)), np.broadcast_to(1.0 - 2.0 * first, (K, N))]).astype(np.float32)
    rows8 = one(np.repeat(np.eye(C), 8, axis=0))
    return {
        "fy_in": fy_in,
        "zp": np.concatenate(halves(place(NIN)), axis=1),
        "fx": np.concatenate(halves(fx), axis=0),
        "masks": masks,
        "pick": pick,
        "rows8": rows8,
        "cols8": np.ascontiguousarray(rows8.T),
        "cols16": one(np.repeat(np.eye(C), 16, axis=1)),
        "rep": rep,
        "ix": np.stack(halves(ix)),
        "owner": owner,
        "iy": iy,
        "iz": halves(back)[0],
        "fy": fy_h,
        "zg": halves(place(8))[0],
        "tile": tile,
    }


FIRST = ("fy_in", "zp", "fx", "masks")


def split(value):
    high = value.astype(BF)
    return high, (value - high.astype(F32)).astype(BF)


def split3(value):
    high = value.astype(BF)
    rest = value - high.astype(F32)
    mid = rest.astype(BF)
    return high, mid, (rest - mid.astype(F32)).astype(BF)


def mm(left, right):
    return jnp.dot(left, right, preferred_element_type=F32)


def nt(left, right):
    return lax.dot_general(left, right, (((1,), (1,)), ((), ())), preferred_element_type=F32)


def right3(high, low, value):
    a, b = split(value)
    return mm(high, a) + mm(high, b) + mm(low, a)


def kernel(dp, slab, names, *refs):
    (prof_in, targ_in, modes_in, local, lift, outw_rows, bias, outb) = refs[:8]
    table_in = dict(zip(names, refs[8 : 8 + len(names)]))
    refs = refs[8 + len(names) :]
    pred_out, grad_out = refs[:2]
    refs = refs[2:]
    table = dict(zip(names, refs[: len(names)]))
    (prof, targ, modes, pred, grad,
     ubuf, sp, rp, sr, rr, wrow, lmat, lt_h, lt_l, kc, wl, pre, sums, spec, lost, bx, sm, rm, b_h,
     line_a, line_b, slope_a, slope_b, off_a, off_b, vbuf, kw, outw, sg, rg, pm, xs, rx,
     in_sem, table_sem, pred_sem, grad_sem, p_send, p_recv, r_send, r_recv, w_send, w_recv, m_send, m_recv, g_send, g_recv, x_send, x_recv) = refs[len(names) :]
    me = lax.axis_index("slab")
    mine = lax.axis_index("dp")
    planes = prof.shape[1]
    share = K // dp
    some = planes // Q
    used = share * K

    barrier = pltpu.get_barrier_semaphore()
    for step in range(1, slab):
        pl.semaphore_signal(barrier, inc=1, device_id={"slab": lax.rem(me + step, slab)}, device_id_type=MESH)
    for step in range(1, dp):
        pl.semaphore_signal(barrier, inc=1, device_id={"dp": lax.rem(mine + step, dp)}, device_id_type=MESH)

    big = [pltpu.make_async_copy(prof_in, prof, in_sem.at[0]), pltpu.make_async_copy(modes_in, modes, in_sem.at[1]), pltpu.make_async_copy(targ_in, targ, in_sem.at[2])]
    small = {n: pltpu.make_async_copy(table_in[n], table[n], table_sem.at[i]) for i, n in enumerate(names)}
    big[0].start()
    for n in FIRST:
        small[n].start()
    big[1].start()
    for n in names:
        if n not in FIRST:
            small[n].start()
    big[2].start()

    def copies(source, target, send, recv, axis, here, count):
        out = []
        for step in range(1, count):
            peer = lax.rem(here + step, count)
            origin = lax.rem(here + count - step, count)

            def make(place, peer=peer):
                return pltpu.make_async_remote_copy(
                    src_ref=source.at[peer], dst_ref=target.at[place], send_sem=send.at[peer], recv_sem=recv.at[place],
                    device_id={axis: peer}, device_id_type=MESH)

            out.append((functools.partial(make, here), functools.partial(make, origin)))
        return out

    def launch(pairs, source, target, here):
        for going, _ in pairs:
            going().start()
        target[pl.ds(here, 1)] = source[pl.ds(here, 1)]

    def finish(pairs):
        for going, coming in pairs:
            coming().wait_recv()
        for going, _ in pairs:
            going().wait_send()

    lane = lax.broadcasted_iota(jnp.int32, (C, N), 1)
    row = lax.broadcasted_iota(jnp.int32, (C, N), 0)

    big[0].wait()
    for n in FIRST:
        small[n].wait()

    @pl.loop(0, planes // 4)
    def _(turn):
        for sub in range(4):
            x = turn * 4 + sub
            rows = pl.ds(pl.multiple_of(x * K, K), K)
            for pair in range(NIN // 2):
                high, low = split(jnp.concatenate([prof[2 * pair, x], prof[2 * pair + 1, x]], axis=1))
                both = mm(table["fy_in"][...], jnp.concatenate([high, low], axis=0))
                u = both[: 2 * K] + both[2 * K :]
                for half in range(2):
                    i = 2 * pair + half
                    lanes = slice(half * N, (half + 1) * N)
                    ubuf[rows, 2 * i * N : (2 * i + 1) * N] = u[:K, lanes]
                    ubuf[rows, (2 * i + 1) * N : (2 * i + 2) * N] = u[K:, lanes]

    high, low = split(ubuf[:, : 2 * NIN * N])
    both = mm(high, table["zp"][...])
    v = both[:, :N] + both[:, N:] + mm(low, table["zp"][:, :N])
    for x in range(planes):
        sp[:, x, :] = v[x * K : (x + 1) * K, :]

    pl.semaphore_wait(barrier, slab + dp - 2)
    pairs = copies(sp, rp, p_send, p_recv, "slab", me, slab)
    launch(pairs, sp, rp, me)

    def groups(scalars):
        out = jnp.where(lane < 3 * C, scalars[2], scalars[3])
        out = jnp.where(lane < 2 * C, scalars[1], out)
        return jnp.where(lane < C, scalars[0], out)

    same = row == lax.rem(lane, C)
    for c in range(C):
        high, low = split(jnp.where(same, groups([lift[i, c] for i in range(NIN)]), 0.0))
        lmat[c * C : (c + 1) * C, :N] = high
        lmat[c * C : (c + 1) * C, N:] = low
    for t in range(C // 4):
        for i in range(NIN):
            high, low = split(jnp.where(same, groups([lift[i, 4 * t + j] for j in range(4)]), 0.0))
            lt_h[i * C : (i + 1) * C, t * N : (t + 1) * N] = high
            lt_l[i * C : (i + 1) * C, t * N : (t + 1) * N] = low
    for n in names:
        if n not in FIRST:
            small[n].wait()
    spread = mm(nt(table["rows8"][...], local[...]).astype(BF), table["cols8"][...])
    wide_lane = lax.broadcasted_iota(jnp.int32, (C * 8, 2 * N), 1)
    wide_row = lax.broadcasted_iota(jnp.int32, (C * 8, 2 * N), 0)
    kc[: C * 8, :] = jnp.where(lax.rem(wide_lane, 8) == lax.rem(wide_row, 8), spread, 0.0).astype(BF)
    kc[C * 8 :, :] = jnp.where(wide_lane[:C] // 8 == wide_row[:C], 1.0, 0.0).astype(BF)
    ones = jnp.ones((N, N), BF)

    def down(value):
        pieces = split3(jnp.where(row == lane, jnp.broadcast_to(value, (C, N)), 0.0))
        return mm(pieces[0], ones) + mm(pieces[1], ones) + mm(pieces[2], ones)

    half_w = outw_rows[...].astype(F32) * 0.5
    for j in range(2):
        column = down(jnp.concatenate([half_w[j : j + 1, :]] * 4, axis=1))
        for o in range(C):
            outw[j, o] = jnp.broadcast_to(column[o : o + 1, :], (16, N)).astype(BF)
    both = jnp.where(row[:, :C] < 16, jnp.broadcast_to(half_w[:1, :], (C, C)), jnp.broadcast_to(half_w[1:, :], (C, C)))
    spread = mm(both.astype(BF), table["cols16"][...])
    wide_lane = lax.broadcasted_iota(jnp.int32, (C, 16 * C), 1)
    wide_row = lax.broadcasted_iota(jnp.int32, (C, 16 * C), 0)
    kw[...] = jnp.where(lax.rem(wide_lane, 16) == lax.rem(wide_row, 16), spread, 0.0).astype(BF)
    sums[...] = jnp.zeros_like(sums)

    def local_map(first, last):
        @pl.loop(first // 4, last // 4)
        def _(turn):
            for sub in range(4):
                step = turn * 4 + sub
                x, yb = step // 8, lax.rem(step, 8)
                sides = []
                for q in range(2):
                    rows = pl.ds(pl.multiple_of(yb * 16 + q * 8, 8), 8)
                    inputs = [prof[i, x, rows, :] for i in range(NIN)]
                    lifted = []
                    for c in range(C):
                        value = lift[0, c] * inputs[0]
                        for i in range(1, NIN):
                            value = value + lift[i, c] * inputs[i]
                        lifted.append(value)
                    sides.append(jnp.concatenate(lifted, axis=0).astype(BF))
                out = mm(kc[...], jnp.concatenate(sides, axis=1))
                pre[x, yb] = out[: C * 8]
                sums[sub] += out[C * 8 :]

    steps = planes * 8
    early = 36
    local_map(0, early)

    big[1].wait()
    for part in range(2):
        for block in range(2):
            rows = slice(block * N, (block + 1) * N)
            total = None
            for t in range(4):
                lanes = slice(t * 2 * N, (t + 1) * 2 * N)
                high, low = split(modes[part, rows, lanes])
                both = mm(high, lmat[lanes, :])
                both = both[:, :N] + both[:, N:] + mm(low, lmat[lanes, :N])
                total = both if total is None else total + both
            wl[part, rows, :] = total

    def weight_row(peer, send):
        return pltpu.make_async_remote_copy(
            src_ref=modes.at[0, pl.ds(0, 1), :], dst_ref=wrow, send_sem=send, recv_sem=w_recv,
            device_id={"slab": peer}, device_id_type=MESH)

    @pl.when(me == 0)
    def _():
        for step in range(1, slab):
            weight_row(step, w_send.at[step]).start()
        wrow[...] = modes[0, :1, :]

    finish(pairs)
    hit = table["masks"][0]
    y = table["fx"]
    y = right3(y[: 2 * K, :], y[2 * K :, :], rp[...].reshape(N, N))
    value = y[:K] + table["masks"][2] * pltpu.roll(y[K:], N // 2, 1)
    constant = (row[:K] == 0) & (lax.rem(lane[:K], K) == 0) & (me == 0)
    spec[...] = jnp.where(constant, 0.0, value)

    def expand(row_of, count):
        wide = jnp.concatenate([jnp.broadcast_to(row_of(p), (K, N)) * hit for p in range(count)], axis=0)
        both = mm(jnp.concatenate(split(wide), axis=1), table["pick"][...])
        return both[:, :N], both[:, N:]

    s_re, s_im = expand(lambda p: spec[p : p + 1, :], K)
    w_re, w_im = wl[0], wl[1]
    spread = []
    for value in (s_re * w_re - s_im * w_im, s_re * w_im + s_im * w_re):
        spread.append(mm(jnp.concatenate(split(value), axis=1), table["rep"][...]))
    keep = jnp.concatenate([hit] * K, axis=0)
    ix_h, ix_l = table["ix"][0], table["ix"][1]
    for og in range(4):
        lanes = slice(og * N, (og + 1) * N)
        re, im = split(spread[0][:, lanes] * keep), split(spread[1][:, lanes] * keep)

        def turned(a, value):
            return mm(ix_h[a], value[0]) + mm(ix_h[a], value[1]) + mm(ix_l[a], value[0])

        for part, out in enumerate((turned(0, re) - turned(1, im), turned(0, im) + turned(1, re))):
            for h in range(Q):
                for d in range(slab):
                    first = d * planes + h * some
                    sm[h, d, :, (2 * og + part) * N : (2 * og + part + 1) * N] = out[first : first + some]

    def moving(h):
        return copies(sm.at[h], rm.at[h], m_send.at[h], m_recv.at[h], "slab", me, slab)

    def leaving(h):
        return copies(sg.at[h], rg.at[h], g_send.at[h], g_recv.at[h], "slab", me, slab)

    for h in range(2):
        launch(moving(h), sm.at[h], rm.at[h], me)
    local_map(early, steps)

    value = (sums[0] + sums[1]) + (sums[2] + sums[3])
    pieces = split3(jnp.concatenate([value[:, :N] + value[:, N:], jnp.zeros((N - C, N), F32)], axis=0))
    flat = jnp.ones((8, N), BF)
    total = nt(flat, pieces[0]) + nt(flat, pieces[1]) + nt(flat, pieces[2])
    for q in range(slab):
        sr[q] = total[:1]
    more = copies(sr, rr, r_send, r_recv, "slab", me, slab)
    launch(more, sr, rr, me)
    for h in range(2, Q):
        launch(moving(h), sm.at[h], rm.at[h], me)

    @pl.when(me == 0)
    def _():
        for step in range(1, slab):
            weight_row(step, w_send.at[step]).wait_send()

    @pl.when(me != 0)
    def _():
        weight_row(0, w_send.at[0]).wait_recv()

    finish(more)
    total = rr[0]
    for q in range(1, slab):
        total = total + rr[q]
    lost[...] = total * jnp.where(me == 0, 1.0 / math.sqrt(N * N * N), 0.0).astype(F32)
    pieces = split3(jnp.broadcast_to(total * (1.0 / (N * N * N)), (8, N)))
    shift = mm(pieces[0], table["owner"][...]) + mm(pieces[1], table["owner"][...]) + mm(pieces[2], table["owner"][...])
    value = jnp.zeros((1, N), F32)
    for t in range(C * C // N):
        lanes = slice(t * N, (t + 1) * N)
        value = value + shift[:1, lanes] * wrow[:, lanes]
    value = value + pltpu.roll(value, 64, 1)
    moved = down(value + pltpu.roll(value, 32, 1))
    top = lax.broadcasted_iota(jnp.int32, (K, N), 0)
    for o in range(C):
        a, b, c = split3(jnp.broadcast_to(moved[o : o + 1, :] + bias[o], (K, N)))
        a, b, c = a.astype(F32), b.astype(F32), c.astype(F32)
        value = jnp.where(top == 0, a, jnp.where(top == 1, b, jnp.where(top == 2, c, 0.0)))
        bx[o // 2, :, (o % 2) * N : (o % 2 + 1) * N] = value.astype(BF)
    big[2].wait()

    c0 = math.sqrt(2.0 / math.pi)

    def lines(rows, pair, out):
        blocks = []
        for half in range(2):
            b = b_h[pair * 2 + half, rows, :]
            blocks.append(jnp.concatenate([b[:, :N], b[:, N:]], axis=0))
        right = jnp.concatenate([jnp.concatenate(blocks, axis=1), bx[pair]], axis=0)
        out[pair] = mm(table["iy"][...], right)

    def activate(x, yb, field, slope, off):
        ys = slice(yb * 16, (yb + 1) * 16)
        hidden = []
        for o in range(C):
            rows = slice(o * 8, (o + 1) * 8)
            base = jnp.concatenate([pre[x, yb, rows, :N], pre[x, yb, rows, N:]], axis=0)
            exact = field[o // 2, ys, (o % 2) * N : (o % 2 + 1) * N] + base
            v = exact.astype(BF)
            a = (exact * c0).astype(BF)
            b = a * ((v * v) * 0.044715)
            t = jnp.tanh(a + b)
            slope[yb, o] = (t + (1.0 - t * t) * ((a + b) + (b + b))) + 1.0
            hidden.append(v + v * t)
        out = mm(kw[...], jnp.concatenate(hidden, axis=0))
        for j in range(2):
            value = out[j * 16 : (j + 1) * 16] + outb[j]
            pred[j, x, ys, :] = value
            off[j, ys, :] = (value - targ[j, x, ys, :]).astype(BF)

    def backward(place, pair, slope, off):
        parts = []
        for half in range(2):
            o = pair * 2 + half
            pieces = []
            for yb in range(N // 16):
                ys = slice(yb * 16, (yb + 1) * 16)
                pieces.append((outw[0, o] * off[0, ys, :] + outw[1, o] * off[1, ys, :]) * slope[yb, o])
            parts.append(jnp.concatenate(pieces, axis=0))
        u = mm(table["fy"][...], jnp.concatenate(parts, axis=1)).astype(BF)
        rows = slice(place * K, (place + 1) * K)
        for half in range(2):
            at = (pair * 2 + half) * 2 * N
            vbuf[rows, at : at + N] = u[:K, half * N : (half + 1) * N]
            vbuf[rows, at + N : at + 2 * N] = u[K:, half * N : (half + 1) * N]

    def pred_copy(x):
        return pltpu.make_async_copy(pred.at[:, x], pred_out.at[:, x], pred_sem.at[x])

    slopes, offs, fields = (slope_a, slope_b), (off_a, off_b), (line_a, line_b)

    @pl.loop(0, Q)
    def _(h):
        finish(moving(h))
        high = jnp.concatenate([rm[h, :, x, og * 2 * N : (og + 1) * 2 * N] for og in range(4) for x in range(some)], axis=0).astype(BF)
        for t in range(8):
            value = mm(high, table["iz"][:, t * 2 * N : (t + 1) * 2 * N]).astype(BF)
            for og in range(4):
                b_h[og * 8 + t] = value[og * some * K : (og + 1) * some * K]
        for pair in range(C // 2):
            lines(slice(0, K), pair, fields[0])
        for x in range(some):
            now, last = x % 2, (x + 1) % 2
            for yb in range(N // 16):
                activate(h * some + x, yb, fields[now], slopes[now], offs[now])
                for pair in (2 * yb, 2 * yb + 1):
                    if x + 1 < some:
                        lines(slice((x + 1) * K, (x + 2) * K), pair, fields[last])
                    if x > 0:
                        backward(x - 1, pair, slopes[last], offs[last])
            pred_copy(h * some + x).start()
        for pair in range(C // 2):
            backward(some - 1, pair, slopes[(some - 1) % 2], offs[(some - 1) % 2])
        v = mm(jnp.concatenate([vbuf[:, og * 16 * N : (og + 1) * 16 * N] for og in range(4)], axis=0), table["zg"][...])
        for og in range(4):
            for x in range(some):
                at = (og * some + x) * K
                sg[h, :, x, og * 2 * N : (og + 1) * 2 * N] = v[at : at + K, :]
        launch(leaving(h), sg.at[h], rg.at[h], me)

    for h in range(Q):
        finish(leaving(h))
        for d in range(slab):
            first = d * planes + h * some
            pm[first : first + some, :] = rg[h, d]

    y = right3(table["fx"][: 2 * K, :], table["fx"][2 * K :, :], pm[...])
    twice = table["masks"][1]
    for og in range(4):
        re, im = slice(2 * og * N, (2 * og + 1) * N), slice((2 * og + 1) * N, (2 * og + 2) * N)
        out_re = (y[:K, re] - y[K:, im]) * twice
        out_im = (y[:K, im] + y[K:, re]) * twice
        for d in range(dp):
            ps = slice(d * share, (d + 1) * share)
            xs[d, :, re] = out_re[ps]
            xs[d, :, im] = out_im[ps]
    for d in range(dp):
        xs[d, :, 8 * N : 9 * N] = spec[d * share : (d + 1) * share, :]
        xs[d, :, 9 * N :] = jnp.broadcast_to(lost[...], (share, N)) if d == 0 else jnp.zeros((share, N), F32)

    pairs = copies(xs, rx, x_send, x_recv, "dp", mine, dp)
    for going, _ in pairs:
        going().start()

    def term(ref, d):
        s_re, s_im = expand(lambda p: ref[d, pl.ds(p, 1), 8 * N : 9 * N], share)
        g = []
        for part in range(2):
            total = None
            for og in range(4):
                at = (2 * og + part) * N
                wide = jnp.concatenate([jnp.broadcast_to(ref[d, pl.ds(p, 1), at : at + N], (K, N)) * hit for p in range(share)], axis=0)
                high, low = split(wide)
                weight = table["tile"][og * N : (og + 1) * N, :]
                value = mm(high, weight) + mm(low, weight)
                total = value if total is None else total + value
            g.append(total)
        pieces = split(jnp.broadcast_to(ref[d, pl.ds(0, 1), 9 * N :], (8, N)))
        gone = (mm(pieces[0], table["owner"][...]) + mm(pieces[1], table["owner"][...]))[:1, :]
        wide = [jnp.concatenate([g[part][:1, :]] * (C * C // N), axis=1) * gone for part in range(2)]
        return s_re * g[0] + s_im * g[1], s_re * g[1] - s_im * g[0], wide[0], wide[1]

    total = term(xs, mine)
    finish(pairs)
    for step in range(1, dp):
        total = [a + b for a, b in zip(total, term(rx, lax.rem(mine + step, dp)))]

    grads = [pltpu.make_async_copy(grad.at[part], grad_out.at[part], grad_sem.at[part]) for part in range(2)]
    for part in range(2):
        high, low = split(total[part])
        value = mm(jnp.concatenate([high, low], axis=1), jnp.concatenate([lt_h[...], lt_h[...]], axis=0)) + mm(high, lt_l[...])
        grad[part] = value
        grad[part, :1, :] = value[:1, :] + total[2 + part]
        grads[part].start()
    for part in range(2):
        grads[part].wait()
    for x in range(planes):
        pred_copy(x).wait()


def body(dp, slab, consts, profiles, target_fields, lift_weight, local_weight, local_bias, output_weight, output_bias, mode_weight):
    planes = profiles.shape[2]
    share = K // dp
    some = planes // Q
    vmem = pl.BlockSpec(memory_space=pltpu.VMEM)
    smem = pl.BlockSpec(memory_space=pltpu.SMEM)
    far = pl.BlockSpec(memory_space=pl.ANY)
    dma = pltpu.SemaphoreType.DMA
    buf = pltpu.VMEM
    names = tuple(consts)
    values = [jnp.asarray(consts[n]) for n in names]
    pred, grad = pl.pallas_call(
        functools.partial(kernel, dp, slab, names),
        out_shape=(jax.ShapeDtypeStruct((2, planes, N, N), F32), jax.ShapeDtypeStruct((2, share * K, C * C), F32)),
        in_specs=[far] * 3 + [vmem, smem, vmem, smem, smem] + [far] * len(names),
        out_specs=(far, far),
        scratch_shapes=[buf(v.shape, v.dtype) for v in values] + [
            buf((NIN, planes, N, N), F32),
            buf((2, planes, N, N), F32),
            buf((2, K * K, C * C), F32),
            buf((2, planes, N, N), F32),
            buf((2, share * K, C * C), F32),
            buf((planes * K, 2 * NIN * N), F32),
            buf((slab, planes, N), F32),
            buf((slab, planes, N), F32),
            buf((slab, 1, N), F32),
            buf((slab, 1, N), F32),
            buf((1, C * C), F32),
            buf((C * C, 2 * N), BF),
            buf((NIN * C, C * C), BF),
            buf((NIN * C, C * C), BF),
            buf((C * 8 + C, 2 * N), BF),
            buf((2, K * K, N), F32),
            buf((planes, N // 16, C * 8, 2 * N), F32),
            buf((4, C, 2 * N), F32),
            buf((K, N), F32),
            buf((1, N), F32),
            buf((C // 2, K, 2 * N), BF),
            buf((Q, slab, some, 8 * N), F32),
            buf((Q, slab, some, 8 * N), F32),
            buf((C, some * K, 2 * N), BF),
            buf((C // 2, N, 2 * N), F32),
            buf((C // 2, N, 2 * N), F32),
            buf((N // 16, C, 16, N), BF),
            buf((N // 16, C, 16, N), BF),
            buf((2, N, N), BF),
            buf((2, N, N), BF),
            buf((some * K, C * 2 * N), BF),
            buf((C, 16 * C), BF),
            buf((2, C, 16, N), BF),
            buf((Q, slab, some, 8 * N), F32),
            buf((Q, slab, some, 8 * N), F32),
            buf((N, 8 * N), F32),
            buf((dp, share, 10 * N), F32),
            buf((dp, share, 10 * N), F32),
            dma((3,)), dma((len(names),)), dma((planes,)), dma((2,)),
            dma((slab,)), dma((slab,)), dma((slab,)), dma((slab,)), dma((slab,)), dma(()),
            dma((Q, slab)), dma((Q, slab)), dma((Q, slab)), dma((Q, slab)), dma((dp,)), dma((dp,)),
        ],
        compiler_params=pltpu.CompilerParams(collective_id=0, has_side_effects=True, vmem_limit_bytes=56 << 20),
    )(profiles[0], target_fields[0], mode_weight.reshape(2, K * K, C * C), local_weight, lift_weight,
      output_weight.T, local_bias, output_bias, *values)
    return pred[None], grad.reshape(2, 1, share, K, C * C)


def solution(mesh):
    consts = tables()
    in_specs = (
        P("dp", None, "slab", None, None),
        P("dp", None, "slab", None, None),
        P(),
        P(),
        P(),
        P(),
        P(),
        P(None, "slab", None, None, None),
    )
    out_specs = (P("dp", None, "slab", None, None), P(None, "slab", "dp", None, None))

    def run(*args):
        return body(mesh.shape["dp"], mesh.shape["slab"], consts, *args)

    return jax.shard_map(run, mesh=mesh, in_specs=in_specs, out_specs=out_specs, check_vma=False)
```

```python
import functools
import math

import jax
import jax.numpy as jnp
import ml_dtypes
import numpy as np
from jax import lax
from jax.experimental import pallas as pl
from jax.experimental.pallas import tpu as pltpu
from jax.sharding import PartitionSpec as P

N = 128
K = 16
C = 32
NIN = 4
Q = 4
MESH = pl.DeviceIdType.MESH
BF = jnp.bfloat16
F32 = jnp.float32


def halves(table):
    table = np.asarray(table, np.float32)
    high = table.astype(ml_dtypes.bfloat16)
    low = (table - high.astype(np.float32)).astype(ml_dtypes.bfloat16)
    return high, low


def tables():
    freq = np.where(np.arange(K) < K // 2, np.arange(K), np.arange(K) - K)
    cell = np.arange(N)
    signed = 2.0 * np.pi * np.mod(freq[:, None] * cell[None, :], N) / N
    plain = 2.0 * np.pi * np.mod(np.arange(K)[:, None] * cell[None, :], N) / N
    norm = 1.0 / math.sqrt(N * N * N)
    doubling = np.where(np.arange(K) == 0, 1.0, 2.0)
    fy_h, fy_l = halves(np.concatenate([np.cos(signed), -np.sin(signed)], axis=0))
    fy_in = np.zeros((4 * K, 2 * N), ml_dtypes.bfloat16)
    fy_in[: 2 * K, :N], fy_in[: 2 * K, N:], fy_in[2 * K :, :N] = fy_h, fy_h, fy_l
    zc, zs = np.cos(plain).T, np.sin(plain).T

    def place(count):
        out = np.zeros((count, 2, N, 2, count, K))
        for c in range(count):
            out[c, 0, :, 0, c], out[c, 0, :, 1, c] = zc, -zs
            out[c, 1, :, 0, c], out[c, 1, :, 1, c] = zs, zc
        return out.reshape(count * 2 * N, 2 * count * K)

    back = np.zeros((2, 8, K, 8, 2, N))
    for c in range(8):
        wc, ws = doubling[:, None] * np.cos(plain), doubling[:, None] * np.sin(plain)
        back[0, c, :, c, 0], back[0, c, :, c, 1] = wc, ws
        back[1, c, :, c, 0], back[1, c, :, c, 1] = -ws, wc
    back = back.reshape(2 * 8 * K, 8 * 2 * N)
    iy = np.zeros((N, 3 * K), ml_dtypes.bfloat16)
    iy[:, : 2 * K] = halves(np.concatenate([np.cos(signed).T, -np.sin(signed).T], axis=1))[0]
    iy[:, 2 * K : 2 * K + 3] = 1.0
    fx = np.concatenate([np.cos(signed), -np.sin(signed)], axis=0) * norm
    ix = np.stack([np.repeat(np.cos(signed).T, K, axis=1), np.repeat(np.sin(signed).T, K, axis=1)]) * norm
    one = lambda value: np.asarray(value, np.float32).astype(ml_dtypes.bfloat16)
    pick = np.zeros((2, 2, NIN, K, 2, NIN, C))
    for part in range(2):
        for i in range(NIN):
            pick[:, part, i, :, part, i, :] = 1.0
    pick = one(pick.reshape(4 * NIN * K, 2 * NIN * C))
    rep = np.zeros((2, NIN, C, C, K))
    tile = np.zeros((C, K, 4, C))
    owner = np.zeros((N, C, C))
    for c in range(C):
        rep[:, :, c, c, :] = 1.0
        tile[c, :, :, c] = 1.0
        owner[c, c, :] = 1.0
    rep = one(rep.reshape(2 * NIN * C, C * K))
    tile = one(tile.reshape(C * K, 4 * C))
    owner = one(owner.reshape(N, C * C))
    hit = np.arange(N)[None, :] % K == np.arange(K)[:, None]
    first = np.arange(N) < N // 2
    masks = np.stack([hit, np.broadcast_to(np.tile(doubling, 8), (K, N)), np.broadcast_to(1.0 - 2.0 * first, (K, N))]).astype(np.float32)
    rows8 = one(np.repeat(np.eye(C), 8, axis=0))
    return {
        "fy_in": fy_in,
        "zp": np.concatenate(halves(place(NIN)), axis=1),
        "fx": np.concatenate(halves(fx), axis=0),
        "masks": masks,
        "pick": pick,
        "rows8": rows8,
        "cols8": np.ascontiguousarray(rows8.T),
        "cols16": one(np.repeat(np.eye(C), 16, axis=1)),
        "rep": rep,
        "ix": np.stack(halves(ix)),
        "owner": owner,
        "iy": iy,
        "iz": columns(halves(back)[0]),
        "fy": fy_h,
        "zg": columns(halves(place(8))[0]),
        "tile": tile,
    }


def columns(table):
    return np.ascontiguousarray(table.reshape(table.shape[0], -1, N).transpose(1, 0, 2))


FIRST = ("fy_in", "zp", "fx", "masks")


def split(value):
    high = value.astype(BF)
    return high, (value - high.astype(F32)).astype(BF)


def split3(value):
    high = value.astype(BF)
    rest = value - high.astype(F32)
    mid = rest.astype(BF)
    return high, mid, (rest - mid.astype(F32)).astype(BF)


def mm(left, right):
    return jnp.dot(left, right, preferred_element_type=F32)


def nt(left, right):
    return lax.dot_general(left, right, (((1,), (1,)), ((), ())), preferred_element_type=F32)


def right3(high, low, value):
    a, b = split(value)
    return mm(high, a) + mm(high, b) + mm(low, a)


def kernel(dp, slab, names, *refs):
    (prof_in, targ_in, modes_in, local, lift, outw_rows, bias, outb) = refs[:8]
    table_in = dict(zip(names, refs[8 : 8 + len(names)]))
    refs = refs[8 + len(names) :]
    pred_out, grad_out = refs[:2]
    refs = refs[2:]
    table = dict(zip(names, refs[: len(names)]))
    (prof, targ, modes, pred, grad,
     ubuf, sp, rp, sr, rr, wrow, lmat, lt_h, lt_l, kc, wl, pre, sums, spec, lost, bx, sm, rm, b_h,
     line_a, line_b, vbuf, kw, outw, sg, rg, pm, xs, rx,
     in_sem, table_sem, pred_sem, grad_sem, p_send, p_recv, r_send, r_recv, w_send, w_recv, m_send, m_recv, g_send, g_recv, x_send, x_recv) = refs[len(names) :]
    me = lax.axis_index("slab")
    mine = lax.axis_index("dp")
    planes = prof.shape[1]
    share = K // dp
    some = planes // Q
    used = share * K

    barrier = pltpu.get_barrier_semaphore()
    for step in range(1, slab):
        pl.semaphore_signal(barrier, inc=1, device_id={"slab": lax.rem(me + step, slab)}, device_id_type=MESH)
    for step in range(1, dp):
        pl.semaphore_signal(barrier, inc=1, device_id={"dp": lax.rem(mine + step, dp)}, device_id_type=MESH)

    big = [pltpu.make_async_copy(prof_in, prof, in_sem.at[0]), pltpu.make_async_copy(modes_in, modes, in_sem.at[1]), pltpu.make_async_copy(targ_in, targ, in_sem.at[2])]
    small = {n: pltpu.make_async_copy(table_in[n], table[n], table_sem.at[i]) for i, n in enumerate(names)}
    big[0].start()
    for n in FIRST:
        small[n].start()
    big[1].start()
    for n in names:
        if n not in FIRST:
            small[n].start()
    big[2].start()

    def launch(source, target, send, recv, axis, here, count):
        for step in range(1, count):
            peer = lax.rem(here + step, count)
            pltpu.make_async_remote_copy(
                src_ref=source.at[peer], dst_ref=target.at[here], send_sem=send, recv_sem=recv,
                device_id={axis: peer}, device_id_type=MESH).start()

    def finish(source, target, send, recv, axis, here, count):
        if count > 1:
            every = pltpu.make_async_remote_copy(
                src_ref=source.at[pl.ds(0, count - 1)], dst_ref=target.at[pl.ds(0, count - 1)], send_sem=send, recv_sem=recv,
                device_id={axis: lax.rem(here + 1, count)}, device_id_type=MESH)
            every.wait_recv()
            every.wait_send()

    def keep_own(source, target, here):
        target[pl.ds(here, 1)] = source[pl.ds(here, 1)]

    lane = lax.broadcasted_iota(jnp.int32, (C, N), 1)
    row = lax.broadcasted_iota(jnp.int32, (C, N), 0)

    big[0].wait()
    for n in FIRST:
        small[n].wait()

    @pl.loop(0, planes // 4)
    def _(turn):
        for sub in range(4):
            x = turn * 4 + sub
            rows = pl.ds(pl.multiple_of(x * K, K), K)
            for pair in range(NIN // 2):
                high, low = split(jnp.concatenate([prof[2 * pair, x], prof[2 * pair + 1, x]], axis=1))
                both = mm(table["fy_in"][...], jnp.concatenate([high, low], axis=0))
                u = both[: 2 * K] + both[2 * K :]
                for half in range(2):
                    i = 2 * pair + half
                    lanes = slice(half * N, (half + 1) * N)
                    ubuf[rows, 2 * i * N : (2 * i + 1) * N] = u[:K, lanes]
                    ubuf[rows, (2 * i + 1) * N : (2 * i + 2) * N] = u[K:, lanes]

    high, low = split(ubuf[:, : 2 * NIN * N])
    both = mm(high, table["zp"][...])
    v = both[:, :N] + both[:, N:] + mm(low, table["zp"][:, :N])
    for x in range(planes):
        sp[:, x, :] = v[x * K : (x + 1) * K, :]

    pl.semaphore_wait(barrier, slab + dp - 2)
    spectra = (sp, rp, p_send, p_recv, "slab", me, slab)
    launch(*spectra)
    keep_own(sp, rp, me)

    def groups(scalars):
        out = jnp.where(lane < 3 * C, scalars[2], scalars[3])
        out = jnp.where(lane < 2 * C, scalars[1], out)
        return jnp.where(lane < C, scalars[0], out)

    same = row == lax.rem(lane, C)
    for c in range(C):
        high, low = split(jnp.where(same, groups([lift[i, c] for i in range(NIN)]), 0.0))
        lmat[c * C : (c + 1) * C, :N] = high
        lmat[c * C : (c + 1) * C, N:] = low
    for t in range(C // 4):
        for i in range(NIN):
            high, low = split(jnp.where(same, groups([lift[i, 4 * t + j] for j in range(4)]), 0.0))
            lt_h[i * C : (i + 1) * C, t * N : (t + 1) * N] = high
            lt_l[i * C : (i + 1) * C, t * N : (t + 1) * N] = low
    for n in names:
        if n not in FIRST:
            small[n].wait()
    spread = mm(nt(table["rows8"][...], local[...]).astype(BF), table["cols8"][...])
    wide_lane = lax.broadcasted_iota(jnp.int32, (C * 8, 2 * N), 1)
    wide_row = lax.broadcasted_iota(jnp.int32, (C * 8, 2 * N), 0)
    kc[: C * 8, :] = jnp.where(lax.rem(wide_lane, 8) == lax.rem(wide_row, 8), spread, 0.0).astype(BF)
    kc[C * 8 :, :] = jnp.where(wide_lane[:C] // 8 == wide_row[:C], 1.0, 0.0).astype(BF)
    ones = jnp.ones((N, N), BF)

    def down(value):
        pieces = split3(jnp.where(row == lane, jnp.broadcast_to(value, (C, N)), 0.0))
        return mm(pieces[0], ones) + mm(pieces[1], ones) + mm(pieces[2], ones)

    half_w = outw_rows[...].astype(F32) * 0.5
    for j in range(2):
        outw[j] = down(jnp.concatenate([half_w[j : j + 1, :]] * 4, axis=1))
    both = jnp.where(row[:, :C] < 16, jnp.broadcast_to(half_w[:1, :], (C, C)), jnp.broadcast_to(half_w[1:, :], (C, C)))
    spread = mm(both.astype(BF), table["cols16"][...])
    wide_lane = lax.broadcasted_iota(jnp.int32, (C, 16 * C), 1)
    wide_row = lax.broadcasted_iota(jnp.int32, (C, 16 * C), 0)
    kw[...] = jnp.where(lax.rem(wide_lane, 16) == lax.rem(wide_row, 16), spread, 0.0).astype(BF)
    sums[...] = jnp.zeros_like(sums)

    def local_map(first, last):
        @pl.loop(first // 4, last // 4)
        def _(turn):
            for sub in range(4):
                step = turn * 4 + sub
                x, yb = step // 8, lax.rem(step, 8)
                sides = []
                for q in range(2):
                    rows = pl.ds(pl.multiple_of(yb * 16 + q * 8, 8), 8)
                    inputs = [prof[i, x, rows, :] for i in range(NIN)]
                    lifted = []
                    for c in range(C):
                        value = lift[0, c] * inputs[0]
                        for i in range(1, NIN):
                            value = value + lift[i, c] * inputs[i]
                        lifted.append(value)
                    sides.append(jnp.concatenate(lifted, axis=0).astype(BF))
                out = mm(kc[...], jnp.concatenate(sides, axis=1))
                pre[x, yb] = out[: C * 8]
                sums[sub] += out[C * 8 :]

    steps = planes * 8
    early = 28
    local_map(0, early)

    big[1].wait()
    for part in range(2):
        for block in range(2):
            rows = slice(block * N, (block + 1) * N)
            total = None
            for t in range(4):
                lanes = slice(t * 2 * N, (t + 1) * 2 * N)
                high, low = split(modes[part, rows, lanes])
                both = mm(high, lmat[lanes, :])
                both = both[:, :N] + both[:, N:] + mm(low, lmat[lanes, :N])
                total = both if total is None else total + both
            wl[part, rows, :] = total

    def weight_row(peer, send):
        return pltpu.make_async_remote_copy(
            src_ref=modes.at[0, pl.ds(0, 1), :], dst_ref=wrow, send_sem=send, recv_sem=w_recv,
            device_id={"slab": peer}, device_id_type=MESH)

    @pl.when(me == 0)
    def _():
        for step in range(1, slab):
            weight_row(step, w_send.at[step]).start()
        wrow[...] = modes[0, :1, :]

    finish(*spectra)
    hit = table["masks"][0]
    y = table["fx"]
    y = right3(y[: 2 * K, :], y[2 * K :, :], rp[...].reshape(N, N))
    value = y[:K] + table["masks"][2] * pltpu.roll(y[K:], N // 2, 1)
    constant = (row[:K] == 0) & (lax.rem(lane[:K], K) == 0) & (me == 0)
    spec[...] = jnp.where(constant, 0.0, value)

    def expand(row_of, count):
        wide = jnp.concatenate([jnp.broadcast_to(row_of(p), (K, N)) * hit for p in range(count)], axis=0)
        both = mm(jnp.concatenate(split(wide), axis=1), table["pick"][...])
        return both[:, :N], both[:, N:]

    s_re, s_im = expand(lambda p: spec[p : p + 1, :], K)
    w_re, w_im = wl[0], wl[1]
    spread = []
    for value in (s_re * w_re - s_im * w_im, s_re * w_im + s_im * w_re):
        spread.append(mm(jnp.concatenate(split(value), axis=1), table["rep"][...]))
    keep = jnp.concatenate([hit] * K, axis=0)
    ix_h, ix_l = table["ix"][0], table["ix"][1]
    for og in range(4):
        lanes = slice(og * N, (og + 1) * N)
        re, im = split(spread[0][:, lanes] * keep), split(spread[1][:, lanes] * keep)

        def turned(a, value):
            return mm(ix_h[a], value[0]) + mm(ix_h[a], value[1]) + mm(ix_l[a], value[0])

        for part, out in enumerate((turned(0, re) - turned(1, im), turned(0, im) + turned(1, re))):
            for h in range(Q):
                for d in range(slab):
                    first = d * planes + h * some
                    sm[h, d, :, (2 * og + part) * N : (2 * og + part + 1) * N] = out[first : first + some]

    def moving(h):
        return sm.at[h], rm.at[h], m_send.at[h], m_recv.at[h], "slab", me, slab

    def leaving(h):
        return sg.at[h], rg.at[h], g_send.at[h], g_recv.at[h], "slab", me, slab

    for h in range(2):
        launch(*moving(h))
        keep_own(sm.at[h], rm.at[h], me)
    local_map(early, steps)

    value = (sums[0] + sums[1]) + (sums[2] + sums[3])
    pieces = split3(jnp.concatenate([value[:, :N] + value[:, N:], jnp.zeros((N - C, N), F32)], axis=0))
    flat = jnp.ones((8, N), BF)
    total = nt(flat, pieces[0]) + nt(flat, pieces[1]) + nt(flat, pieces[2])
    for q in range(slab):
        sr[q] = total[:1]
    more = (sr, rr, r_send, r_recv, "slab", me, slab)
    launch(*more)
    keep_own(sr, rr, me)
    for h in range(2, Q):
        launch(*moving(h))
        keep_own(sm.at[h], rm.at[h], me)

    @pl.when(me == 0)
    def _():
        for step in range(1, slab):
            weight_row(step, w_send.at[step]).wait_send()

    @pl.when(me != 0)
    def _():
        weight_row(0, w_send.at[0]).wait_recv()

    finish(*more)
    total = rr[0]
    for q in range(1, slab):
        total = total + rr[q]
    lost[...] = total * jnp.where(me == 0, 1.0 / math.sqrt(N * N * N), 0.0).astype(F32)
    pieces = split3(jnp.broadcast_to(total * (1.0 / (N * N * N)), (8, N)))
    shift = mm(pieces[0], table["owner"][...]) + mm(pieces[1], table["owner"][...]) + mm(pieces[2], table["owner"][...])
    value = jnp.zeros((1, N), F32)
    for t in range(C * C // N):
        lanes = slice(t * N, (t + 1) * N)
        value = value + shift[:1, lanes] * wrow[:, lanes]
    value = value + pltpu.roll(value, 64, 1)
    moved = down(value + pltpu.roll(value, 32, 1))
    top = lax.broadcasted_iota(jnp.int32, (K, N), 0)
    for o in range(C):
        a, b, c = split3(jnp.broadcast_to(moved[o : o + 1, :] + bias[o], (K, N)))
        a, b, c = a.astype(F32), b.astype(F32), c.astype(F32)
        value = jnp.where(top == 0, a, jnp.where(top == 1, b, jnp.where(top == 2, c, 0.0)))
        bx[o // 2, :, (o % 2) * N : (o % 2 + 1) * N] = value
    big[2].wait()

    c0 = math.sqrt(2.0 / math.pi)

    def lines(rows, pair, out):
        blocks = []
        for half in range(2):
            b = b_h[pair * 2 + half, rows, :]
            blocks.append(jnp.concatenate([b[:, :N], b[:, N:]], axis=0))
        right = jnp.concatenate([jnp.concatenate(blocks, axis=1), bx[pair]], axis=0).astype(BF)
        out[pair] = mm(table["iy"][...], right)

    def activate(x, yb, field):
        ys = slice(yb * 16, (yb + 1) * 16)
        hidden, slope, off = [], [], []
        for o in range(C):
            rows = slice(o * 8, (o + 1) * 8)
            base = jnp.concatenate([pre[x, yb, rows, :N], pre[x, yb, rows, N:]], axis=0)
            exact = field[o // 2, ys, (o % 2) * N : (o % 2 + 1) * N] + base
            v = exact.astype(BF)
            a = (exact * c0).astype(BF)
            b = a * ((v * v) * 0.044715)
            both = a + b
            t = jnp.tanh(both)
            slope.append((t + (1.0 - t * t) * (both + (b + b))) + 1.0)
            hidden.append(v + v * t)
        out = mm(kw[...], jnp.concatenate(hidden, axis=0))
        for j in range(2):
            value = out[j * 16 : (j + 1) * 16] + outb[j]
            pred[j, x, ys, :] = value
            off.append((value - targ[j, x, ys, :]).astype(BF))
        return slope, off

    def backward(place, pair, saved):
        parts = []
        for half in range(2):
            o = pair * 2 + half
            w = [jnp.broadcast_to(outw[j, o : o + 1, :], (16, N)).astype(BF) for j in range(2)]
            pieces = [(w[0] * off[0] + w[1] * off[1]) * slope[o] for slope, off in saved]
            parts.append(jnp.concatenate(pieces, axis=0))
        u = mm(table["fy"][...], jnp.concatenate(parts, axis=1))
        rows = slice(place * K, (place + 1) * K)
        for half in range(2):
            at = (pair * 2 + half) * 2 * N
            vbuf[rows, at : at + N] = u[:K, half * N : (half + 1) * N]
            vbuf[rows, at + N : at + 2 * N] = u[K:, half * N : (half + 1) * N]

    def pred_copy(x):
        return pltpu.make_async_copy(pred.at[:, x], pred_out.at[:, x], pred_sem.at[x])

    fields = (line_a, line_b)

    @pl.loop(0, Q)
    def _(h):
        finish(*moving(h))
        high = jnp.concatenate([rm[h, :, x, og * 2 * N : (og + 1) * 2 * N] for og in range(4) for x in range(some)], axis=0).astype(BF)
        for t in range(8):
            value = mm(high, jnp.concatenate([table["iz"][2 * t], table["iz"][2 * t + 1]], axis=1))
            for og in range(4):
                b_h[og * 8 + t] = value[og * some * K : (og + 1) * some * K]
        for pair in range(C // 2):
            lines(slice(0, K), pair, fields[0])
        before = None
        for x in range(some):
            saved = []
            for yb in range(N // 16):
                saved.append(activate(h * some + x, yb, fields[x % 2]))
                for pair in (2 * yb, 2 * yb + 1):
                    if x + 1 < some:
                        lines(slice((x + 1) * K, (x + 2) * K), pair, fields[(x + 1) % 2])
                    if x > 0:
                        backward(x - 1, pair, before)
            pred_copy(h * some + x).start()
            before = saved
        for pair in range(C // 2):
            backward(some - 1, pair, before)
        left = jnp.concatenate([vbuf[:, og * 16 * N : (og + 1) * 16 * N] for og in range(4)], axis=0).astype(BF)
        v = mm(left, jnp.concatenate([table["zg"][0], table["zg"][1]], axis=1))
        for og in range(4):
            for x in range(some):
                at = (og * some + x) * K
                sg[h, :, x, og * 2 * N : (og + 1) * 2 * N] = v[at : at + K, :]
        launch(*leaving(h))
        keep_own(sg.at[h], rg.at[h], me)

    for h in range(Q):
        finish(*leaving(h))
        for d in range(slab):
            first = d * planes + h * some
            pm[first : first + some, :] = rg[h, d]

    y = right3(table["fx"][: 2 * K, :], table["fx"][2 * K :, :], pm[...])
    twice = table["masks"][1]
    for og in range(4):
        re, im = slice(2 * og * N, (2 * og + 1) * N), slice((2 * og + 1) * N, (2 * og + 2) * N)
        out_re = (y[:K, re] - y[K:, im]) * twice
        out_im = (y[:K, im] + y[K:, re]) * twice
        for d in range(dp):
            ps = slice(d * share, (d + 1) * share)
            xs[d, :, re] = out_re[ps]
            xs[d, :, im] = out_im[ps]
    for d in range(dp):
        xs[d, :, 8 * N : 9 * N] = spec[d * share : (d + 1) * share, :]
        xs[d, :, 9 * N :] = jnp.broadcast_to(lost[...], (share, N)) if d == 0 else jnp.zeros((share, N), F32)

    across = (xs, rx, x_send, x_recv, "dp", mine, dp)
    launch(*across)

    def term(ref, d):
        s_re, s_im = expand(lambda p: ref[d, pl.ds(p, 1), 8 * N : 9 * N], share)
        g = []
        for part in range(2):
            total = None
            for og in range(4):
                at = (2 * og + part) * N
                wide = jnp.concatenate([jnp.broadcast_to(ref[d, pl.ds(p, 1), at : at + N], (K, N)) * hit for p in range(share)], axis=0)
                high, low = split(wide)
                weight = table["tile"][og * N : (og + 1) * N, :]
                value = mm(high, weight) + mm(low, weight)
                total = value if total is None else total + value
            g.append(total)
        pieces = split(jnp.broadcast_to(ref[d, pl.ds(0, 1), 9 * N :], (8, N)))
        gone = (mm(pieces[0], table["owner"][...]) + mm(pieces[1], table["owner"][...]))[:1, :]
        wide = [jnp.concatenate([g[part][:1, :]] * (C * C // N), axis=1) * gone for part in range(2)]
        return s_re * g[0] + s_im * g[1], s_re * g[1] - s_im * g[0], wide[0], wide[1]

    total = term(xs, mine)
    finish(*across)
    for step in range(1, dp):
        total = [a + b for a, b in zip(total, term(rx, lax.rem(mine + step, dp)))]

    grads = [pltpu.make_async_copy(grad.at[part], grad_out.at[part], grad_sem.at[part]) for part in range(2)]
    for part in range(2):
        high, low = split(total[part])
        value = mm(jnp.concatenate([high, low], axis=1), jnp.concatenate([lt_h[...], lt_h[...]], axis=0)) + mm(high, lt_l[...])
        grad[part] = value
        grad[part, :1, :] = value[:1, :] + total[2 + part]
        grads[part].start()
    for part in range(2):
        grads[part].wait()
    for x in range(planes):
        pred_copy(x).wait()


def body(dp, slab, consts, profiles, target_fields, lift_weight, local_weight, local_bias, output_weight, output_bias, mode_weight):
    planes = profiles.shape[2]
    share = K // dp
    some = planes // Q
    vmem = pl.BlockSpec(memory_space=pltpu.VMEM)
    smem = pl.BlockSpec(memory_space=pltpu.SMEM)
    far = pl.BlockSpec(memory_space=pl.ANY)
    dma = pltpu.SemaphoreType.DMA
    buf = pltpu.VMEM
    names = tuple(consts)
    values = [jnp.asarray(consts[n]) for n in names]
    pred, grad = pl.pallas_call(
        functools.partial(kernel, dp, slab, names),
        out_shape=(jax.ShapeDtypeStruct((2, planes, N, N), F32), jax.ShapeDtypeStruct((2, share * K, C * C), F32)),
        in_specs=[far] * 3 + [vmem, smem, vmem, smem, smem] + [far] * len(names),
        out_specs=(far, far),
        scratch_shapes=[buf(v.shape, v.dtype) for v in values] + [
            buf((NIN, planes, N, N), F32),
            buf((2, planes, N, N), F32),
            buf((2, K * K, C * C), F32),
            buf((2, planes, N, N), F32),
            buf((2, share * K, C * C), F32),
            buf((planes * K, 2 * NIN * N), F32),
            buf((slab, planes, N), F32),
            buf((slab, planes, N), F32),
            buf((slab, 1, N), F32),
            buf((slab, 1, N), F32),
            buf((1, C * C), F32),
            buf((C * C, 2 * N), BF),
            buf((NIN * C, C * C), BF),
            buf((NIN * C, C * C), BF),
            buf((C * 8 + C, 2 * N), BF),
            buf((2, K * K, N), F32),
            buf((planes, N // 16, C * 8, 2 * N), F32),
            buf((4, C, 2 * N), F32),
            buf((K, N), F32),
            buf((1, N), F32),
            buf((C // 2, K, 2 * N), F32),
            buf((Q, slab, some, 8 * N), F32),
            buf((Q, slab, some, 8 * N), F32),
            buf((C, some * K, 2 * N), F32),
            buf((C // 2, N, 2 * N), F32),
            buf((C // 2, N, 2 * N), F32),
            buf((some * K, C * 2 * N), F32),
            buf((C, 16 * C), BF),
            buf((2, C, N), F32),
            buf((Q, slab, some, 8 * N), F32),
            buf((Q, slab, some, 8 * N), F32),
            buf((N, 8 * N), F32),
            buf((dp, share, 10 * N), F32),
            buf((dp, share, 10 * N), F32),
            dma((3,)), dma((len(names),)), dma((planes,)), dma((2,)),
            dma(()), dma(()), dma(()), dma(()), dma((slab,)), dma(()),
            dma((Q,)), dma((Q,)), dma((Q,)), dma((Q,)), dma(()), dma(()),
        ],
        compiler_params=pltpu.CompilerParams(collective_id=0, has_side_effects=True, vmem_limit_bytes=56 << 20),
    )(profiles[0], target_fields[0], mode_weight.reshape(2, K * K, C * C), local_weight, lift_weight,
      output_weight.T, local_bias, output_bias, *values)
    return pred[None], grad.reshape(2, 1, share, K, C * C)


def solution(mesh):
    consts = tables()
    in_specs = (
        P("dp", None, "slab", None, None),
        P("dp", None, "slab", None, None),
        P(),
        P(),
        P(),
        P(),
        P(),
        P(None, "slab", None, None, None),
    )
    out_specs = (P("dp", None, "slab", None, None), P(None, "slab", "dp", None, None))

    def run(*args):
        return body(mesh.shape["dp"], mesh.shape["slab"], consts, *args)

    return jax.shard_map(run, mesh=mesh, in_specs=in_specs, out_specs=out_specs, check_vma=False)
```

```python
import functools
import math

import jax
import jax.numpy as jnp
import ml_dtypes
import numpy as np
from jax import lax
from jax.experimental import pallas as pl
from jax.experimental.pallas import tpu as pltpu
from jax.sharding import PartitionSpec as P

N = 128
K = 16
C = 32
NIN = 4
Q = 4
MESH = pl.DeviceIdType.MESH
BF = jnp.bfloat16
F32 = jnp.float32


def halves(table):
    table = np.asarray(table, np.float32)
    high = table.astype(ml_dtypes.bfloat16)
    low = (table - high.astype(np.float32)).astype(ml_dtypes.bfloat16)
    return high, low


def tables():
    freq = np.where(np.arange(K) < K // 2, np.arange(K), np.arange(K) - K)
    cell = np.arange(N)
    signed = 2.0 * np.pi * np.mod(freq[:, None] * cell[None, :], N) / N
    plain = 2.0 * np.pi * np.mod(np.arange(K)[:, None] * cell[None, :], N) / N
    norm = 1.0 / math.sqrt(N * N * N)
    doubling = np.where(np.arange(K) == 0, 1.0, 2.0)
    fy_h, fy_l = halves(np.concatenate([np.cos(signed), -np.sin(signed)], axis=0))
    fy_in = np.zeros((4 * K, 2 * N), ml_dtypes.bfloat16)
    fy_in[: 2 * K, :N], fy_in[: 2 * K, N:], fy_in[2 * K :, :N] = fy_h, fy_h, fy_l
    zc, zs = np.cos(plain).T, np.sin(plain).T

    def place(count):
        out = np.zeros((count, 2, N, 2, count, K))
        for c in range(count):
            out[c, 0, :, 0, c], out[c, 0, :, 1, c] = zc, -zs
            out[c, 1, :, 0, c], out[c, 1, :, 1, c] = zs, zc
        return out.reshape(count * 2 * N, 2 * count * K)

    back = np.zeros((2, 8, K, 8, 2, N))
    for c in range(8):
        wc, ws = doubling[:, None] * np.cos(plain), doubling[:, None] * np.sin(plain)
        back[0, c, :, c, 0], back[0, c, :, c, 1] = wc, ws
        back[1, c, :, c, 0], back[1, c, :, c, 1] = -ws, wc
    back = back.reshape(2 * 8 * K, 8 * 2 * N)
    iy = np.zeros((N, 3 * K), ml_dtypes.bfloat16)
    iy[:, : 2 * K] = halves(np.concatenate([np.cos(signed).T, -np.sin(signed).T], axis=1))[0]
    iy[:, 2 * K : 2 * K + 3] = 1.0
    fx = np.concatenate([np.cos(signed), -np.sin(signed)], axis=0) * norm
    ix = np.stack([np.repeat(np.cos(signed).T, K, axis=1), np.repeat(np.sin(signed).T, K, axis=1)]) * norm
    one = lambda value: np.asarray(value, np.float32).astype(ml_dtypes.bfloat16)
    pick = np.zeros((2, 2, NIN, K, 2, NIN, C))
    for part in range(2):
        for i in range(NIN):
            pick[:, part, i, :, part, i, :] = 1.0
    pick = one(pick.reshape(4 * NIN * K, 2 * NIN * C))
    rep = np.zeros((2, NIN, C, C, K))
    tile = np.zeros((C, K, 4, C))
    owner = np.zeros((N, C, C))
    for c in range(C):
        rep[:, :, c, c, :] = 1.0
        tile[c, :, :, c] = 1.0
        owner[c, c, :] = 1.0
    rep = one(rep.reshape(2 * NIN * C, C * K))
    tile = one(tile.reshape(C * K, 4 * C))
    owner = one(owner.reshape(N, C * C))
    hit = np.arange(N)[None, :] % K == np.arange(K)[:, None]
    first = np.arange(N) < N // 2
    masks = np.stack([hit, np.broadcast_to(np.tile(doubling, 8), (K, N)), np.broadcast_to(1.0 - 2.0 * first, (K, N))]).astype(np.float32)
    rows8 = one(np.repeat(np.eye(C), 8, axis=0))
    return {
        "fy_in": fy_in,
        "zp": np.concatenate(halves(place(NIN)), axis=1),
        "fx": np.concatenate(halves(fx), axis=0),
        "masks": masks,
        "pick": pick,
        "rows8": rows8,
        "cols8": np.ascontiguousarray(rows8.T),
        "cols16": one(np.repeat(np.eye(C), 16, axis=1)),
        "rep": rep,
        "ix": np.stack(halves(ix)),
        "owner": owner,
        "iy": iy,
        "iz": columns(halves(back)[0]),
        "fy": fy_h,
        "zg": columns(halves(place(8))[0]),
        "tile": tile,
    }


def columns(table):
    return np.ascontiguousarray(table.reshape(table.shape[0], -1, N).transpose(1, 0, 2))


FIRST = ("fy_in", "zp", "fx", "masks")


def split(value):
    high = value.astype(BF)
    return high, (value - high.astype(F32)).astype(BF)


def split3(value):
    high = value.astype(BF)
    rest = value - high.astype(F32)
    mid = rest.astype(BF)
    return high, mid, (rest - mid.astype(F32)).astype(BF)


def mm(left, right):
    return jnp.dot(left, right, preferred_element_type=F32)


def nt(left, right):
    return lax.dot_general(left, right, (((1,), (1,)), ((), ())), preferred_element_type=F32)


def right3(high, low, value):
    a, b = split(value)
    return mm(high, a) + mm(high, b) + mm(low, a)


def kernel(dp, slab, names, *refs):
    (prof_in, targ_in, modes_in, local, lift, outw_rows, bias, outb) = refs[:8]
    table_in = dict(zip(names, refs[8 : 8 + len(names)]))
    refs = refs[8 + len(names) :]
    pred_out, grad_out = refs[:2]
    refs = refs[2:]
    table = dict(zip(names, refs[: len(names)]))
    (prof, targ, modes, pred, grad,
     ubuf, sp, rp, sr, rr, wrow, lmat, lt_h, lt_l, kc, kd, wl, raised, sums, spec, lost, bx, sm, rm, b_h,
     line_a, line_b, vbuf, kw, outw, sg, rg, pm, xs, rx,
     in_sem, table_sem, pred_sem, grad_sem, p_send, p_recv, r_send, r_recv, w_send, w_recv, m_send, m_recv, g_send, g_recv, x_send, x_recv) = refs[len(names) :]
    me = lax.axis_index("slab")
    mine = lax.axis_index("dp")
    planes = prof.shape[1]
    share = K // dp
    some = planes // Q
    used = share * K

    barrier = pltpu.get_barrier_semaphore()
    for step in range(1, slab):
        pl.semaphore_signal(barrier, inc=1, device_id={"slab": lax.rem(me + step, slab)}, device_id_type=MESH)
    for step in range(1, dp):
        pl.semaphore_signal(barrier, inc=1, device_id={"dp": lax.rem(mine + step, dp)}, device_id_type=MESH)

    big = [pltpu.make_async_copy(prof_in, prof, in_sem.at[0]), pltpu.make_async_copy(modes_in, modes, in_sem.at[1]), pltpu.make_async_copy(targ_in, targ, in_sem.at[2])]
    small = {n: pltpu.make_async_copy(table_in[n], table[n], table_sem.at[i]) for i, n in enumerate(names)}
    big[0].start()
    for n in FIRST:
        small[n].start()
    big[1].start()
    for n in names:
        if n not in FIRST:
            small[n].start()
    big[2].start()

    def launch(source, target, send, recv, axis, here, count):
        for step in range(1, count):
            peer = lax.rem(here + step, count)
            pltpu.make_async_remote_copy(
                src_ref=source.at[peer], dst_ref=target.at[here], send_sem=send, recv_sem=recv,
                device_id={axis: peer}, device_id_type=MESH).start()

    def finish(source, target, send, recv, axis, here, count):
        if count > 1:
            every = pltpu.make_async_remote_copy(
                src_ref=source.at[pl.ds(0, count - 1)], dst_ref=target.at[pl.ds(0, count - 1)], send_sem=send, recv_sem=recv,
                device_id={axis: lax.rem(here + 1, count)}, device_id_type=MESH)
            every.wait_recv()
            every.wait_send()

    def keep_own(source, target, here):
        target[pl.ds(here, 1)] = source[pl.ds(here, 1)]

    lane = lax.broadcasted_iota(jnp.int32, (C, N), 1)
    row = lax.broadcasted_iota(jnp.int32, (C, N), 0)

    big[0].wait()
    for n in FIRST:
        small[n].wait()

    @pl.loop(0, planes // 4)
    def _(turn):
        for sub in range(4):
            x = turn * 4 + sub
            rows = pl.ds(pl.multiple_of(x * K, K), K)
            for pair in range(NIN // 2):
                high, low = split(jnp.concatenate([prof[2 * pair, x], prof[2 * pair + 1, x]], axis=1))
                both = mm(table["fy_in"][...], jnp.concatenate([high, low], axis=0))
                u = both[: 2 * K] + both[2 * K :]
                for half in range(2):
                    i = 2 * pair + half
                    lanes = slice(half * N, (half + 1) * N)
                    ubuf[rows, 2 * i * N : (2 * i + 1) * N] = u[:K, lanes]
                    ubuf[rows, (2 * i + 1) * N : (2 * i + 2) * N] = u[K:, lanes]

    high, low = split(ubuf[:, : 2 * NIN * N])
    both = mm(high, table["zp"][...])
    v = both[:, :N] + both[:, N:] + mm(low, table["zp"][:, :N])
    for x in range(planes):
        sp[:, x, :] = v[x * K : (x + 1) * K, :]

    pl.semaphore_wait(barrier, slab + dp - 2)
    spectra = (sp, rp, p_send, p_recv, "slab", me, slab)
    launch(*spectra)
    keep_own(sp, rp, me)

    def groups(scalars):
        out = jnp.where(lane < 3 * C, scalars[2], scalars[3])
        out = jnp.where(lane < 2 * C, scalars[1], out)
        return jnp.where(lane < C, scalars[0], out)

    same = row == lax.rem(lane, C)
    for c in range(C):
        high, low = split(jnp.where(same, groups([lift[i, c] for i in range(NIN)]), 0.0))
        lmat[c * C : (c + 1) * C, :N] = high
        lmat[c * C : (c + 1) * C, N:] = low
    for t in range(C // 4):
        for i in range(NIN):
            high, low = split(jnp.where(same, groups([lift[i, 4 * t + j] for j in range(4)]), 0.0))
            lt_h[i * C : (i + 1) * C, t * N : (t + 1) * N] = high
            lt_l[i * C : (i + 1) * C, t * N : (t + 1) * N] = low
    for n in names:
        if n not in FIRST:
            small[n].wait()
    spread = mm(nt(table["rows8"][...], local[...]).astype(BF), table["cols8"][...])
    wide_lane = lax.broadcasted_iota(jnp.int32, (C * 8, 2 * N), 1)
    wide_row = lax.broadcasted_iota(jnp.int32, (C * 8, 2 * N), 0)
    spread = jnp.where(lax.rem(wide_lane, 8) == lax.rem(wide_row, 8), spread, 0.0).astype(BF)
    owned = jnp.where(wide_lane[:C] // 8 == wide_row[:C], 1.0, 0.0).astype(BF)
    for q in range(2):
        kc[q] = spread[:, q * N : (q + 1) * N]
        kd[q] = owned[:, q * N : (q + 1) * N]
    ones = jnp.ones((N, N), BF)

    def down(value):
        pieces = split3(jnp.where(row == lane, jnp.broadcast_to(value, (C, N)), 0.0))
        return mm(pieces[0], ones) + mm(pieces[1], ones) + mm(pieces[2], ones)

    half_w = outw_rows[...].astype(F32) * 0.5
    for j in range(2):
        outw[j] = down(jnp.concatenate([half_w[j : j + 1, :]] * 4, axis=1))
    both = jnp.where(row[:, :C] < 16, jnp.broadcast_to(half_w[:1, :], (C, C)), jnp.broadcast_to(half_w[1:, :], (C, C)))
    spread = mm(both.astype(BF), table["cols16"][...])
    wide_lane = lax.broadcasted_iota(jnp.int32, (C, 16 * C), 1)
    wide_row = lax.broadcasted_iota(jnp.int32, (C, 16 * C), 0)
    spread = jnp.where(lax.rem(wide_lane, 16) == lax.rem(wide_row, 16), spread, 0.0).astype(BF)
    for q in range(4):
        kw[q] = spread[:, q * N : (q + 1) * N]
    sums[...] = jnp.zeros_like(sums)

    def lift_cells(first, last):
        @pl.loop(first // 4, last // 4)
        def _(turn):
            for sub in range(4):
                step = turn * 4 + sub
                x, yb = step // 8, lax.rem(step, 8)
                sides = []
                for q in range(2):
                    rows = pl.ds(pl.multiple_of(yb * 16 + q * 8, 8), 8)
                    inputs = [prof[i, x, rows, :] for i in range(NIN)]
                    lifted = []
                    for c in range(C):
                        value = lift[0, c] * inputs[0]
                        for i in range(1, NIN):
                            value = value + lift[i, c] * inputs[i]
                        lifted.append(value)
                    sides.append(jnp.concatenate(lifted, axis=0).astype(BF))
                    raised[step, q] = sides[q]
                sums[sub] += mm(jnp.concatenate([kd[0], kd[1]], axis=1), jnp.concatenate(sides, axis=1))

    steps = planes * 8
    early = 32
    lift_cells(0, early)

    big[1].wait()
    for part in range(2):
        for block in range(2):
            rows = slice(block * N, (block + 1) * N)
            total = None
            for t in range(4):
                lanes = slice(t * 2 * N, (t + 1) * 2 * N)
                high, low = split(modes[part, rows, lanes])
                both = mm(high, lmat[lanes, :])
                both = both[:, :N] + both[:, N:] + mm(low, lmat[lanes, :N])
                total = both if total is None else total + both
            wl[part, rows, :] = total

    def weight_row(peer, send):
        return pltpu.make_async_remote_copy(
            src_ref=modes.at[0, pl.ds(0, 1), :], dst_ref=wrow, send_sem=send, recv_sem=w_recv,
            device_id={"slab": peer}, device_id_type=MESH)

    @pl.when(me == 0)
    def _():
        for step in range(1, slab):
            weight_row(step, w_send.at[step]).start()
        wrow[...] = modes[0, :1, :]

    finish(*spectra)
    hit = table["masks"][0]
    y = table["fx"]
    y = right3(y[: 2 * K, :], y[2 * K :, :], rp[...].reshape(N, N))
    value = y[:K] + table["masks"][2] * pltpu.roll(y[K:], N // 2, 1)
    constant = (row[:K] == 0) & (lax.rem(lane[:K], K) == 0) & (me == 0)
    spec[...] = jnp.where(constant, 0.0, value)

    def expand(row_of, count):
        wide = jnp.concatenate([jnp.broadcast_to(row_of(p), (K, N)) * hit for p in range(count)], axis=0)
        both = mm(jnp.concatenate(split(wide), axis=1), table["pick"][...])
        return both[:, :N], both[:, N:]

    s_re, s_im = expand(lambda p: spec[p : p + 1, :], K)
    w_re, w_im = wl[0], wl[1]
    spread = []
    for value in (s_re * w_re - s_im * w_im, s_re * w_im + s_im * w_re):
        spread.append(mm(jnp.concatenate(split(value), axis=1), table["rep"][...]))
    keep = jnp.concatenate([hit] * K, axis=0)
    ix_h, ix_l = table["ix"][0], table["ix"][1]
    for og in range(4):
        lanes = slice(og * N, (og + 1) * N)
        re, im = split(spread[0][:, lanes] * keep), split(spread[1][:, lanes] * keep)

        def turned(a, value):
            return mm(ix_h[a], value[0]) + mm(ix_h[a], value[1]) + mm(ix_l[a], value[0])

        for part, out in enumerate((turned(0, re) - turned(1, im), turned(0, im) + turned(1, re))):
            for h in range(Q):
                for d in range(slab):
                    first = d * planes + h * some
                    sm[h, d, :, (2 * og + part) * N : (2 * og + part + 1) * N] = out[first : first + some]

    def moving(h):
        return sm.at[h], rm.at[h], m_send.at[h], m_recv.at[h], "slab", me, slab

    def leaving(h):
        return sg.at[h], rg.at[h], g_send.at[h], g_recv.at[h], "slab", me, slab

    launch(*moving(0))
    keep_own(sm.at[0], rm.at[0], me)
    lift_cells(early, steps)

    value = (sums[0] + sums[1]) + (sums[2] + sums[3])
    pieces = split3(jnp.concatenate([value[:, :N] + value[:, N:], jnp.zeros((N - C, N), F32)], axis=0))
    flat = jnp.ones((8, N), BF)
    total = nt(flat, pieces[0]) + nt(flat, pieces[1]) + nt(flat, pieces[2])
    for q in range(slab):
        sr[q] = total[:1]
    more = (sr, rr, r_send, r_recv, "slab", me, slab)
    launch(*more)
    keep_own(sr, rr, me)
    for h in range(1, Q):
        launch(*moving(h))
        keep_own(sm.at[h], rm.at[h], me)

    @pl.when(me == 0)
    def _():
        for step in range(1, slab):
            weight_row(step, w_send.at[step]).wait_send()

    @pl.when(me != 0)
    def _():
        weight_row(0, w_send.at[0]).wait_recv()

    finish(*more)
    total = rr[0]
    for q in range(1, slab):
        total = total + rr[q]
    lost[...] = total * jnp.where(me == 0, 1.0 / math.sqrt(N * N * N), 0.0).astype(F32)
    pieces = split3(jnp.broadcast_to(total * (1.0 / (N * N * N)), (8, N)))
    shift = mm(pieces[0], table["owner"][...]) + mm(pieces[1], table["owner"][...]) + mm(pieces[2], table["owner"][...])
    value = jnp.zeros((1, N), F32)
    for t in range(C * C // N):
        lanes = slice(t * N, (t + 1) * N)
        value = value + shift[:1, lanes] * wrow[:, lanes]
    value = value + pltpu.roll(value, 64, 1)
    moved = down(value + pltpu.roll(value, 32, 1))
    top = lax.broadcasted_iota(jnp.int32, (K, N), 0)
    for o in range(C):
        a, b, c = split3(jnp.broadcast_to(moved[o : o + 1, :] + bias[o], (K, N)))
        a, b, c = a.astype(F32), b.astype(F32), c.astype(F32)
        value = jnp.where(top == 0, a, jnp.where(top == 1, b, jnp.where(top == 2, c, 0.0)))
        bx[o // 2, :, (o % 2) * N : (o % 2 + 1) * N] = value
    big[2].wait()

    c0 = math.sqrt(2.0 / math.pi)

    def lines(rows, pair, out):
        blocks = []
        for half in range(2):
            b = b_h[pair * 2 + half, rows, :]
            blocks.append(jnp.concatenate([b[:, :N], b[:, N:]], axis=0))
        right = jnp.concatenate([jnp.concatenate(blocks, axis=1), bx[pair]], axis=0).astype(BF)
        out[pair] = mm(table["iy"][...], right)

    def local_map(x, yb):
        step = x * (N // 16) + yb
        return mm(jnp.concatenate([kc[0], kc[1]], axis=1), jnp.concatenate([raised[step, 0], raised[step, 1]], axis=1))

    def activate(x, yb, field, local_part):
        ys = slice(yb * 16, (yb + 1) * 16)
        hidden, slope, off = [], [], []
        for o in range(C):
            rows = slice(o * 8, (o + 1) * 8)
            base = jnp.concatenate([local_part[rows, :N], local_part[rows, N:]], axis=0)
            exact = field[o // 2, ys, (o % 2) * N : (o % 2 + 1) * N] + base
            v = exact.astype(BF)
            a = (exact * c0).astype(BF)
            b = a * ((v * v) * 0.044715)
            both = a + b
            t = jnp.tanh(both)
            slope.append((t + (1.0 - t * t) * (both + (b + b))) + 1.0)
            hidden.append(v + v * t)
        out = mm(jnp.concatenate([kw[q] for q in range(4)], axis=1), jnp.concatenate(hidden, axis=0))
        for j in range(2):
            value = out[j * 16 : (j + 1) * 16] + outb[j]
            pred[j, x, ys, :] = value
            off.append((value - targ[j, x, ys, :]).astype(BF))
        return slope, off

    def backward(place, pair, saved):
        parts = []
        for half in range(2):
            o = pair * 2 + half
            w = [jnp.broadcast_to(outw[j, o : o + 1, :], (16, N)).astype(BF) for j in range(2)]
            pieces = [(w[0] * off[0] + w[1] * off[1]) * slope[o] for slope, off in saved]
            parts.append(jnp.concatenate(pieces, axis=0))
        u = mm(table["fy"][...], jnp.concatenate(parts, axis=1))
        rows = slice(place * K, (place + 1) * K)
        for half in range(2):
            at = (pair * 2 + half) * 2 * N
            vbuf[rows, at : at + N] = u[:K, half * N : (half + 1) * N]
            vbuf[rows, at + N : at + 2 * N] = u[K:, half * N : (half + 1) * N]

    def pred_copy(x):
        return pltpu.make_async_copy(pred.at[:, x], pred_out.at[:, x], pred_sem.at[x])

    fields = (line_a, line_b)

    def inverse(h):
        high = jnp.concatenate([rm[h, :, x, og * 2 * N : (og + 1) * 2 * N] for og in range(4) for x in range(some)], axis=0).astype(BF)
        for t in range(8):
            value = mm(high, jnp.concatenate([table["iz"][2 * t], table["iz"][2 * t + 1]], axis=1))
            for og in range(4):
                b_h[og * 8 + t] = value[og * some * K : (og + 1) * some * K]

    @pl.loop(0, Q)
    def _(h):
        ahead = local_map(h * some, 0)
        finish(*moving(h))
        inverse(h)
        for pair in range(C // 2):
            lines(slice(0, K), pair, fields[0])
        before = None
        for x in range(some):
            saved = []
            for yb in range(N // 16):
                ready = ahead
                if yb + 1 < N // 16:
                    ahead = local_map(h * some + x, yb + 1)
                elif x + 1 < some:
                    ahead = local_map(h * some + x + 1, 0)
                saved.append(activate(h * some + x, yb, fields[x % 2], ready))
                for pair in (2 * yb, 2 * yb + 1):
                    if x + 1 < some:
                        lines(slice((x + 1) * K, (x + 2) * K), pair, fields[(x + 1) % 2])
                    if x > 0:
                        backward(x - 1, pair, before)
            pred_copy(h * some + x).start()
            before = saved
        for pair in range(C // 2):
            backward(some - 1, pair, before)
        left = jnp.concatenate([vbuf[:, og * 16 * N : (og + 1) * 16 * N] for og in range(4)], axis=0).astype(BF)
        v = mm(left, jnp.concatenate([table["zg"][0], table["zg"][1]], axis=1))
        for og in range(4):
            for x in range(some):
                at = (og * some + x) * K
                sg[h, :, x, og * 2 * N : (og + 1) * 2 * N] = v[at : at + K, :]
        launch(*leaving(h))
        keep_own(sg.at[h], rg.at[h], me)

    for h in range(Q):
        finish(*leaving(h))
        for d in range(slab):
            first = d * planes + h * some
            pm[first : first + some, :] = rg[h, d]

    y = right3(table["fx"][: 2 * K, :], table["fx"][2 * K :, :], pm[...])
    twice = table["masks"][1]
    for og in range(4):
        re, im = slice(2 * og * N, (2 * og + 1) * N), slice((2 * og + 1) * N, (2 * og + 2) * N)
        out_re = (y[:K, re] - y[K:, im]) * twice
        out_im = (y[:K, im] + y[K:, re]) * twice
        for d in range(dp):
            ps = slice(d * share, (d + 1) * share)
            xs[d, :, re] = out_re[ps]
            xs[d, :, im] = out_im[ps]
    for d in range(dp):
        xs[d, :, 8 * N : 9 * N] = spec[d * share : (d + 1) * share, :]
        xs[d, :, 9 * N :] = jnp.broadcast_to(lost[...], (share, N)) if d == 0 else jnp.zeros((share, N), F32)

    across = (xs, rx, x_send, x_recv, "dp", mine, dp)
    launch(*across)

    def term(ref, d):
        s_re, s_im = expand(lambda p: ref[d, pl.ds(p, 1), 8 * N : 9 * N], share)
        g = []
        for part in range(2):
            total = None
            for og in range(4):
                at = (2 * og + part) * N
                wide = jnp.concatenate([jnp.broadcast_to(ref[d, pl.ds(p, 1), at : at + N], (K, N)) * hit for p in range(share)], axis=0)
                high, low = split(wide)
                weight = table["tile"][og * N : (og + 1) * N, :]
                value = mm(high, weight) + mm(low, weight)
                total = value if total is None else total + value
            g.append(total)
        pieces = split(jnp.broadcast_to(ref[d, pl.ds(0, 1), 9 * N :], (8, N)))
        gone = (mm(pieces[0], table["owner"][...]) + mm(pieces[1], table["owner"][...]))[:1, :]
        wide = [jnp.concatenate([g[part][:1, :]] * (C * C // N), axis=1) * gone for part in range(2)]
        return s_re * g[0] + s_im * g[1], s_re * g[1] - s_im * g[0], wide[0], wide[1]

    total = term(xs, mine)
    finish(*across)
    for step in range(1, dp):
        total = [a + b for a, b in zip(total, term(rx, lax.rem(mine + step, dp)))]

    grads = [pltpu.make_async_copy(grad.at[part], grad_out.at[part], grad_sem.at[part]) for part in range(2)]
    for part in range(2):
        high, low = split(total[part])
        value = mm(jnp.concatenate([high, low], axis=1), jnp.concatenate([lt_h[...], lt_h[...]], axis=0)) + mm(high, lt_l[...])
        grad[part] = value
        grad[part, :1, :] = value[:1, :] + total[2 + part]
        grads[part].start()
    for part in range(2):
        grads[part].wait()
    for x in range(planes):
        pred_copy(x).wait()


def body(dp, slab, consts, profiles, target_fields, lift_weight, local_weight, local_bias, output_weight, output_bias, mode_weight):
    planes = profiles.shape[2]
    share = K // dp
    some = planes // Q
    vmem = pl.BlockSpec(memory_space=pltpu.VMEM)
    smem = pl.BlockSpec(memory_space=pltpu.SMEM)
    far = pl.BlockSpec(memory_space=pl.ANY)
    dma = pltpu.SemaphoreType.DMA
    buf = pltpu.VMEM
    names = tuple(consts)
    values = [jnp.asarray(consts[n]) for n in names]
    pred, grad = pl.pallas_call(
        functools.partial(kernel, dp, slab, names),
        out_shape=(jax.ShapeDtypeStruct((2, planes, N, N), F32), jax.ShapeDtypeStruct((2, share * K, C * C), F32)),
        in_specs=[far] * 3 + [vmem, smem, vmem, smem, smem] + [far] * len(names),
        out_specs=(far, far),
        scratch_shapes=[buf(v.shape, v.dtype) for v in values] + [
            buf((NIN, planes, N, N), F32),
            buf((2, planes, N, N), F32),
            buf((2, K * K, C * C), F32),
            buf((2, planes, N, N), F32),
            buf((2, share * K, C * C), F32),
            buf((planes * K, 2 * NIN * N), F32),
            buf((slab, planes, N), F32),
            buf((slab, planes, N), F32),
            buf((slab, 1, N), F32),
            buf((slab, 1, N), F32),
            buf((1, C * C), F32),
            buf((C * C, 2 * N), BF),
            buf((NIN * C, C * C), BF),
            buf((NIN * C, C * C), BF),
            buf((2, C * 8, N), BF),
            buf((2, C, N), BF),
            buf((2, K * K, N), F32),
            buf((planes * (N // 16), 2, C * 8, N), BF),
            buf((4, C, 2 * N), F32),
            buf((K, N), F32),
            buf((1, N), F32),
            buf((C // 2, K, 2 * N), F32),
            buf((Q, slab, some, 8 * N), F32),
            buf((Q, slab, some, 8 * N), F32),
            buf((C, some * K, 2 * N), F32),
            buf((C // 2, N, 2 * N), F32),
            buf((C // 2, N, 2 * N), F32),
            buf((some * K, C * 2 * N), F32),
            buf((4, C, N), BF),
            buf((2, C, N), F32),
            buf((Q, slab, some, 8 * N), F32),
            buf((Q, slab, some, 8 * N), F32),
            buf((N, 8 * N), F32),
            buf((dp, share, 10 * N), F32),
            buf((dp, share, 10 * N), F32),
            dma((3,)), dma((len(names),)), dma((planes,)), dma((2,)),
            dma(()), dma(()), dma(()), dma(()), dma((slab,)), dma(()),
            dma((Q,)), dma((Q,)), dma((Q,)), dma((Q,)), dma(()), dma(()),
        ],
        compiler_params=pltpu.CompilerParams(collective_id=0, has_side_effects=True, vmem_limit_bytes=56 << 20),
    )(profiles[0], target_fields[0], mode_weight.reshape(2, K * K, C * C), local_weight, lift_weight,
      output_weight.T, local_bias, output_bias, *values)
    return pred[None], grad.reshape(2, 1, share, K, C * C)


def solution(mesh):
    consts = tables()
    in_specs = (
        P("dp", None, "slab", None, None),
        P("dp", None, "slab", None, None),
        P(),
        P(),
        P(),
        P(),
        P(),
        P(None, "slab", None, None, None),
    )
    out_specs = (P("dp", None, "slab", None, None), P(None, "slab", "dp", None, None))

    def run(*args):
        return body(mesh.shape["dp"], mesh.shape["slab"], consts, *args)

    return jax.shard_map(run, mesh=mesh, in_specs=in_specs, out_specs=out_specs, check_vma=False)
```
